256 devices in a mesh: aux: 32 (over y_hi, z, core), vir: 8 (over x, y_lo).
Axes of the slice: x: 4, y: 4 (y_hi: 2, y_lo: 2; y = y_hi * 2 + y_lo), z: 8, core: 2. Of those that a mesh axis runs over, the one named last changes fastest.
Arguments:
- b_ov: bfloat16 [128, 2048, 512], P('aux', 'vir'), may hold values from -0.00390625 to 0.00390625
- b_vv: bfloat16 [128, 2048, 2048], P('aux', 'vir'), may hold values from -0.125 to 0.125
- b_oo: bfloat16 [128, 512, 512], P('aux'), may hold values from -0.03125 to 0.03125
- rhs: float32 [2048, 512], P('vir'), may hold values from -6 to 6
- fit_pert: float32 [128], P('aux'), may hold values from -6 to 6
- eps_vir: float32 [2048], P('vir'), may hold values from 1 to 3
- eps_occ: float32 [512], replicated, may hold values from -2 to -1
Outputs:
- response: float32 [2048, 512], P('vir')
The draws below stay inside these ranges and needn't reach their ends.
All inputs are finite; a program needn't handle non-finite values.
Results may differ from the reference program's by a relative error of at most 0.006.
Values may be sent and summed in bfloat16 or wider, within the bound.
No kernel may reach another device: no remote copies, remote signals or barrier semaphores. Data moves between devices by JAX's collectives and lax.ppermute only.
A program may use at most 64 MiB of HBM per device.

```python
import math
import jax
import jax.numpy as jnp
from jax import lax

V = 2048
O = 512
ITERS = 3
NAUX = 128


def block_scale(own_key, extent, cuts, least, high):
    factor_of, own = 1.0, jax.random.fold_in(own_key, 6)
    for position, blocks in cuts:
        steps = jnp.exp(jax.random.uniform(jax.random.fold_in(own, position), (blocks,), jnp.float32, least / len(cuts), high / len(cuts)))
        factor_of = factor_of * jnp.repeat(steps, extent[position] // blocks).reshape([-1 if axis == position else 1 for axis in range(len(extent))])
    return factor_of


def centred(stream_key, dims, spread, limit, cuts=(), kind=jnp.bfloat16):
    values = spread * jax.random.normal(stream_key, dims, jnp.float32)
    if cuts:
        values = values * block_scale(stream_key, dims, cuts, -0.22, 0.18)
    return jnp.clip(values, -limit, limit).astype(kind)


def setup_inputs(seed: int = 0) -> dict:
    splits = jax.random.split(jax.random.key(seed), 8)
    b_ov = centred(splits[0], (NAUX, V, O), (2 * V * O) ** -0.5, 0.00390625, ((0, 32), (1, 8)))
    b_vv = centred(splits[1], (NAUX, V, V), V ** -0.5, 0.125, ((0, 32), (1, 8)))
    b_oo = centred(splits[2], (NAUX, O, O), (O * NAUX // 2) ** -0.5, 0.03125, ((0, 32),))
    rhs = centred(splits[3], (V, O), 1.0, 6.0, ((0, 8),), jnp.float32)
    fit_pert = centred(splits[4], (NAUX,), 1.0, 6.0, ((0, 32),), jnp.float32)
    eps_vir = jnp.clip(1.0 + 2.0 * jax.random.uniform(splits[5], (V,), jnp.float32) ** block_scale(splits[5], (V,), ((0, 8),), -0.2, 0.2), 1.0, 3.0)
    eps_occ = jnp.clip(jax.random.uniform(splits[6], (O,), jnp.float32, -2.0, -1.0), -2.0, -1.0)
    return dict(b_ov=b_ov, b_vv=b_vv, b_oo=b_oo, rhs=rhs, fit_pert=fit_pert, eps_vir=eps_vir, eps_occ=eps_occ)


def reference(b_ov, b_vv, b_oo, rhs, fit_pert, eps_vir, eps_occ):
    scale = math.sqrt(4.0 * V * O / NAUX)
    denom = eps_vir[:, None] - eps_occ[None, :]
    current = (rhs / denom).astype(jnp.bfloat16)
    result = rhs
    for step in range(ITERS):

        def one_aux(total, items):
            pair_ov, pair_vv, pair_oo, pert = items
            fitted = jnp.sum(pair_ov.astype(jnp.float32) * current.astype(jnp.float32))
            weight = scale * pert - 4.0 * fitted
            mixed = jnp.dot(pair_vv, current, preferred_element_type=jnp.float32).astype(jnp.bfloat16)
            term = jnp.dot(mixed, pair_oo, preferred_element_type=jnp.float32)
            return (total + weight * pair_ov.astype(jnp.float32) + term, None)
        total, _ = lax.scan(one_aux, jnp.zeros((V, O), jnp.float32), (b_ov, b_vv, b_oo, fit_pert))
        result = (rhs + total) / denom
        if step < ITERS - 1:
            current = result.astype(jnp.bfloat16)
    return result
```

```python
import math

import jax
import jax.numpy as jnp
from jax import lax
from jax.sharding import Mesh
from jax.sharding import PartitionSpec as P

V = 2048
O = 512
NAUX = 128
ITERS = 3
AUX = ("yh", "z", "c")
VIR = ("x", "yl")
PLANE = ("x", "yl", "yh")
SCALE = math.sqrt(4.0 * V * O / NAUX)
BF, F32 = jnp.bfloat16, jnp.float32


def swap(value, axis, bit=1):
    n = lax.axis_size(axis)
    return lax.ppermute(value, axis, [(i, i ^ bit) for i in range(n)])


def sent_to_all(value, axes, n):
    wide = jnp.broadcast_to(value[None], (n, *value.shape))
    return lax.all_to_all(wide, axes, 0, 0, tiled=True)


def half(value, which, dim):
    size = value.shape[dim] // 2
    return lax.dynamic_slice_in_dim(value, which * size, size, dim)


def local(b_ov, b_vv, b_oo, rhs, fit_pert, eps_vir, eps_occ):
    c = lax.axis_index("c")
    yh = lax.axis_index("yh")
    block = lax.axis_index("x") * 2 + lax.axis_index("yl")
    rhs_part = half(half(rhs, c, 1), yh, 0)
    denom_part = half(eps_vir, yh, 0)[:, None] - half(eps_occ, c, 0)[None, :]
    vv = (b_vv, swap(b_vv, "c"))
    oo = (half(b_oo, c, 1), swap(half(b_oo, 1 - c, 1), "c"))
    ov = jnp.concatenate([half(b_ov, c, 2), swap(half(b_ov, 1 - c, 2), "c")])
    fit = jnp.concatenate([fit_pert, swap(fit_pert, "c")])
    part = rhs_part / denom_part
    for step in range(ITERS):
        full = sent_to_all(part.astype(BF), PLANE, 16).reshape(V, O // 2)
        own = lax.dynamic_slice_in_dim(full, block * 256, 256, 0)
        fitted = jnp.sum(ov.astype(F32) * own.astype(F32)[None], axis=(1, 2))
        fitted = fitted + jnp.roll(swap(fitted, "c"), 4)
        fitted = fitted + swap(fitted, "yl")
        fitted = fitted + swap(fitted, "x", 1)
        fitted = fitted + swap(fitted, "x", 2)
        weight = SCALE * fit - 4.0 * fitted
        total = jnp.zeros((rhs.shape[0], O), F32)
        for vvs, oos in zip(vv, oo, strict=True):
            mixed = jnp.einsum("qab,bj->qaj", vvs, full, preferred_element_type=F32)
            total = total + jnp.einsum(
                "qaj,qji->ai", mixed.astype(BF), oos, preferred_element_type=F32
            )
        extra = jnp.sum(ov.astype(F32) * weight[:, None, None], axis=0)
        chip = half(total, c, 1) + extra + swap(half(total, 1 - c, 1), "c")
        rows = half(chip, yh, 0) + swap(half(chip, 1 - yh, 0).astype(BF), "yh")
        share = sent_to_all(rows.astype(BF), "z", 8).astype(F32).sum(axis=0)
        part = (rhs_part + share) / denom_part
    part = part.astype(BF)
    there = swap(part, "yh")
    both = jnp.where(yh == 0, jnp.stack([part, there]), jnp.stack([there, part]))
    both = both.reshape(2 * part.shape[0], part.shape[1])
    there = swap(both, "c")
    left, right = jnp.where(c == 0, both, there), jnp.where(c == 0, there, both)
    return jnp.concatenate([left, right], axis=1).astype(F32)


def solution(mesh):
    split = Mesh(mesh.devices.reshape(2, 8, 2, 4, 2), ("yh", "z", "c", "x", "yl"))
    placed = (
        P(AUX, VIR, None),
        P(AUX, VIR, None),
        P(AUX, None, None),
        P(VIR, None),
        P(AUX),
        P(VIR),
        P(),
    )
    return jax.shard_map(
        local, mesh=split, in_specs=placed, out_specs=P(VIR, None), check_vma=False
    )
```

```python
import functools
import math

import jax
import jax.numpy as jnp
from jax import lax
from jax.experimental import pallas as pl
from jax.experimental.pallas import tpu as pltpu
from jax.sharding import Mesh
from jax.sharding import PartitionSpec as P

V = 2048
O = 512
NAUX = 128
ITERS = 3
AUX = ("yh", "z", "c")
VIR = ("x", "yl")
PLANE = ("x", "yl", "yh")
SCALE = math.sqrt(4.0 * V * O / NAUX)
BF, F32 = jnp.bfloat16, jnp.float32
ROWS, COLS, GROWS = 128, 256, 16
PIECE = ROWS + GROWS


def sds(*shape, dtype=F32):
    return jax.ShapeDtypeStruct(shape, dtype)


def whole(*shape):
    return pl.BlockSpec(shape, lambda i, s: (0,) * len(shape))


def kernel(body, name, inputs, outputs, scratch=(), limit=16, flops=0):
    specs = [
        whole(*shape) if index is None else pl.BlockSpec(shape, index)
        for shape, index in inputs
    ]
    moved = sum(math.prod(o.shape) * o.dtype.itemsize for o in outputs)
    moved += sum(2 * math.prod(shape) for shape, _ in inputs)
    return pl.pallas_call(
        body,
        out_shape=list(outputs),
        grid_spec=pltpu.PrefetchScalarGridSpec(
            num_scalar_prefetch=1,
            grid=(1,),
            in_specs=specs,
            out_specs=[whole(*o.shape) for o in outputs],
            scratch_shapes=list(scratch),
        ),
        compiler_params=pltpu.CompilerParams(vmem_limit_bytes=limit << 20),
        cost_estimate=pl.CostEstimate(
            flops=flops, bytes_accessed=moved, transcendentals=0
        ),
        name=name,
    )


def at(index, size):
    return pl.ds(pl.multiple_of(index * size, size), size)


def fill(msg, body, sums, first):
    g = jnp.sum(sums, axis=1, keepdims=True)
    high = g.astype(BF)
    low = (g - high.astype(F32)).astype(BF)
    n = sums.shape[0]
    block = jnp.concatenate(
        [jnp.broadcast_to(high, (n, 128)), jnp.broadcast_to(low, (n, 128))], axis=1
    )
    for p in range(16):
        msg[p, :ROWS, :] = body
        if n == GROWS:
            msg[p, ROWS:, :] = block
        else:
            msg[p, ROWS:, :] = first(block)


def start_body(s, rhs, ev, eo, ov, msg, keep):
    c, yh = s[0], s[1]
    u = (rhs[...] / (ev[...] - eo[...])).astype(BF)
    keep[...] = u
    wide = u.astype(F32)
    rows = [
        jnp.sum(ov[q].astype(F32) * wide, axis=0, keepdims=True) for q in range(4)
    ]
    sums = jnp.concatenate([r[:, :COLS] + r[:, COLS:] for r in rows], axis=0)
    sums = jnp.concatenate([sums, jnp.zeros((4, COLS), F32)], axis=0)
    zero = jnp.zeros_like(sums)
    sums = jnp.concatenate(
        [jnp.where(yh == 0, sums, zero), jnp.where(yh == 0, zero, sums)], axis=0
    )
    fill(msg, keep[at(yh, ROWS), at(c, COLS)], sums, None)


def pack_body(s, ov, ov2, ov8, out):
    c, yh = s[0], s[1]
    for k, ref in enumerate((ov, ov2)):
        for q in range(4):
            ov8[k * 4 + q] = ref[q, :, at(c, COLS)]
            out[k * 4 + q] = ref[q, at(1 - yh, ROWS), at(c, COLS)]


def main_body(s, v1, v2, o1, o2, u, keep, send, gown, full, zs, gs):
    c, yh = s[0], s[1]
    g = jnp.zeros((GROWS, COLS), F32)
    for p in range(16):
        full[p * ROWS : (p + 1) * ROWS, :] = u[p, :ROWS, :]
        g = g + u[p, ROWS:, :].astype(F32)
    gs[...] = g[:, :128] + g[:, 128:]
    gown[...] = gs[at(yh, 8), :]
    for k, v in enumerate((v1, v2)):
        z = jnp.dot(
            v[...].reshape(4 * 256, V), full[...], preferred_element_type=F32
        ).astype(BF)
        for q in range(4):
            zs[:, (k * 4 + q) * 256 : (k * 4 + q + 1) * 256] = z[q * 256 : (q + 1) * 256]
    a = jnp.zeros((256, COLS), F32)
    b = jnp.zeros((256, COLS), F32)
    for k, o in enumerate((o1, o2)):
        for q in range(4):
            zq = zs[:, (k * 4 + q) * 256 : (k * 4 + q + 1) * 256]
            a += jnp.dot(zq, o[q, :, at(c, COLS)], preferred_element_type=F32)
            b += jnp.dot(zq, o[q, :, at(1 - c, COLS)], preferred_element_type=F32)
    keep[...] = a
    send[...] = b


def pair_body(s, keep, got, gown, gsw, fit, ov8, mine, other, tot):
    yh = s[1]
    g = gown[...] + jnp.concatenate([gsw[4:8, :], gsw[0:4, :]], axis=0)
    w = SCALE * fit[...] - 4.0 * g
    for h in range(2):
        lanes = slice(h * 128, (h + 1) * 128)
        acc = keep[:, lanes] + got[:, lanes]
        for q in range(8):
            acc += ov8[q, :, lanes].astype(F32) * w[q : q + 1, :]
        tot[:, lanes] = acc
    mine[...] = tot[at(yh, ROWS), :]
    other[...] = tot[at(1 - yh, ROWS), :].astype(BF)


def wide_body(s, mine, recv, out):
    total = (mine[...] + recv[...].astype(F32)).astype(BF)
    for p in range(8):
        out[p] = total


def updated(zm, rhs, ev, eo):
    share = zm[0].astype(F32)
    for p in range(1, 8):
        share += zm[p].astype(F32)
    return (rhs[...] + share) / (ev[...] - eo[...])


def update_body(s, zm, rhs, ev, eo, own, oth, msg, sums):
    yh = s[1]
    u = updated(zm, rhs, ev, eo).astype(BF)
    wide = u.astype(F32)
    for ref, first in ((own, yh), (oth, 1 - yh)):
        rows = [
            jnp.sum(ref[q].astype(F32) * wide, axis=0, keepdims=True) for q in range(8)
        ]
        sums[at(first, 8), :] = jnp.concatenate(rows, axis=0)
    fill(msg, u, sums[...], None)


def last_body(s, zm, rhs, ev, eo, out):
    out[...] = updated(zm, rhs, ev, eo)


def join_body(s, w, wy, wc, wyc, out):
    c, yh = s[0], s[1]
    out[at(yh, ROWS), at(c, COLS)] = w[...]
    out[at(1 - yh, ROWS), at(c, COLS)] = wy[...]
    out[at(yh, ROWS), at(1 - c, COLS)] = wc[...]
    out[at(1 - yh, ROWS), at(1 - c, COLS)] = wyc[...]


def swap(value, axis):
    return lax.ppermute(value, axis, [(0, 1), (1, 0)])


def quarter(i, s):
    return (s[1], s[0])


def local(b_ov, b_vv, b_oo, rhs, fit_pert, eps_vir, eps_occ):
    s = jnp.stack([lax.axis_index("c"), lax.axis_index("yh")]).astype(jnp.int32)
    ev, eo = eps_vir[:, None], eps_occ[None, :]
    msg = kernel(
        start_body,
        "start",
        [((256, O), None), ((256, 1), None), ((1, O), None), ((4, 256, O), None)],
        [sds(16, PIECE, COLS, dtype=BF)],
        [pltpu.VMEM((256, O), BF)],
    )(s, rhs, ev, eo, b_ov)[0]
    vv2, oo2, ov2 = swap(b_vv, "c"), swap(b_oo, "c"), swap(b_ov, "c")
    fit = jnp.concatenate([fit_pert, swap(fit_pert, "c")])
    fit = jnp.broadcast_to(fit[:, None], (8, 128))
    ov8, ov_out = kernel(
        pack_body,
        "pack",
        [((4, 256, O), None)] * 2,
        [sds(8, 256, COLS, dtype=BF), sds(8, ROWS, COLS, dtype=BF)],
    )(s, b_ov, ov2)
    ov_in = None
    denominators = [
        ((ROWS, COLS), quarter),
        ((ROWS, 1), lambda i, s: (s[1], 0)),
        ((1, COLS), lambda i, s: (0, s[0])),
    ]
    for step in range(ITERS):
        msg = lax.all_to_all(msg, PLANE, 0, 0, tiled=True)
        if ov_in is None:
            ov_in = swap(ov_out, "yh")
        half_oo = ((4, 256, O), lambda i, s: (0, s[0], 0))
        keep, send, gown = kernel(
            main_body,
            "main",
            [((4, 256, V), None)] * 2 + [half_oo] * 2 + [((16, PIECE, COLS), None)],
            [sds(256, COLS), sds(256, COLS), sds(8, 128)],
            [
                pltpu.VMEM((V, COLS), BF),
                pltpu.VMEM((256, V), BF),
                pltpu.VMEM((GROWS, 128), F32),
            ],
            limit=32,
            flops=2 * 8 * 256 * 256 * (V + O),
        )(s, b_vv, vv2, b_oo, oo2, msg)
        mine, other = kernel(
            pair_body,
            "pair",
            [((256, COLS), None)] * 2 + [((8, 128), None)] * 3 + [((8, 256, COLS), None)],
            [sds(ROWS, COLS), sds(ROWS, COLS, dtype=BF)],
            [pltpu.VMEM((256, COLS), F32)],
        )(s, keep, swap(send, "c"), gown, swap(gown, "c"), fit, ov8)
        zm = kernel(
            wide_body,
            "wide",
            [((ROWS, COLS), None)] * 2,
            [sds(8, ROWS, COLS, dtype=BF)],
        )(s, mine, swap(other, "yh"))[0]
        zm = lax.all_to_all(zm, "z", 0, 0, tiled=True)
        if step < ITERS - 1:
            msg = kernel(
                update_body,
                "update",
                [((8, ROWS, COLS), None), *denominators]
                + [((8, ROWS, COLS), lambda i, s: (0, s[1], 0)), ((8, ROWS, COLS), None)],
                [sds(16, PIECE, COLS, dtype=BF)],
                [pltpu.VMEM((GROWS, COLS), F32)],
            )(s, zm, rhs, ev, eo, ov8, ov_in)[0]
    w = kernel(
        last_body,
        "last",
        [((8, ROWS, COLS), None), *denominators],
        [sds(ROWS, COLS)],
    )(s, zm, rhs, ev, eo)[0]
    wy, wc = swap(w, "yh"), swap(w, "c")
    return kernel(
        join_body, "join", [((ROWS, COLS), None)] * 4, [sds(256, O)]
    )(s, w, wy, wc, swap(wy, "c"))[0]


def solution(mesh):
    split = Mesh(mesh.devices.reshape(2, 8, 2, 4, 2), ("yh", "z", "c", "x", "yl"))
    placed = (
        P(AUX, VIR, None),
        P(AUX, VIR, None),
        P(AUX, None, None),
        P(VIR, None),
        P(AUX),
        P(VIR),
        P(),
    )
    return jax.shard_map(
        local, mesh=split, in_specs=placed, out_specs=P(VIR, None), check_vma=False
    )
```

```python
import math

import jax
import jax.numpy as jnp
from jax import lax
from jax.experimental import pallas as pl
from jax.experimental.pallas import tpu as pltpu
from jax.sharding import Mesh
from jax.sharding import PartitionSpec as P

V = 2048
O = 512
NAUX = 128
ITERS = 3
AUX = ("yh", "z", "c")
VIR = ("x", "yl")
PLANE = ("x", "yl", "yh")
SCALE = math.sqrt(4.0 * V * O / NAUX)
BF, F32 = jnp.bfloat16, jnp.float32
ROWS, COLS, GROWS = 128, 256, 8
PIECE = ROWS + GROWS


def sds(*shape, dtype=F32):
    return jax.ShapeDtypeStruct(shape, dtype)


def kernel(body, name, outputs, scratch=(), limit=8, flops=0, scalars=1):
    def call(*args):
        moved = sum(math.prod(a.shape) * a.dtype.itemsize for a in (*args, *outputs))
        return pl.pallas_call(
            body,
            out_shape=list(outputs),
            in_specs=[
                pl.BlockSpec(memory_space=pltpu.SMEM if k < scalars else pltpu.VMEM)
                for k in range(len(args))
            ],
            out_specs=[pl.BlockSpec(memory_space=pltpu.VMEM) for _ in outputs],
            scratch_shapes=list(scratch),
            compiler_params=pltpu.CompilerParams(vmem_limit_bytes=limit << 20),
            cost_estimate=pl.CostEstimate(
                flops=flops, bytes_accessed=moved, transcendentals=0
            ),
            name=name,
        )(*args)

    return call


def at(index, size):
    return pl.ds(pl.multiple_of(index * size, size), size)


def spread(sums):
    g = jnp.sum(sums, axis=1, keepdims=True)
    high = g.astype(BF)
    low = (g - high.astype(F32)).astype(BF)
    lane = lax.broadcasted_iota(jnp.int32, (GROWS, 128), 1)
    wide = (GROWS, 128)
    return jnp.where(
        lane % 2 == 0,
        jnp.broadcast_to(high.astype(F32), wide),
        jnp.broadcast_to(low.astype(F32), wide),
    )


def send_all(msg, body, left, right):
    block = jnp.concatenate([left, right], axis=1).astype(BF)
    for p in range(16):
        msg[p, :ROWS, :] = body
        msg[p, ROWS:, :] = block


def lane_sums(refs, wide):
    return jnp.concatenate(
        [jnp.sum(v.astype(F32) * wide, axis=0, keepdims=True) for v in refs], axis=0
    )


def start_body(s, rhs, ev, eo, ov, msg, ovs, rq, dq, keep, den):
    c, yh = s[0], s[1]
    column = jnp.broadcast_to(ev[...], (128, 256)).T
    for h in range(4):
        lanes = slice(h * 128, (h + 1) * 128)
        den[:, lanes] = column - eo[:, lanes]
    u = (rhs[...] / den[...]).astype(BF)
    keep[...] = u
    rq[...] = rhs[at(yh, ROWS), at(c, COLS)]
    dq[...] = den[at(yh, ROWS), at(c, COLS)]
    sums = lane_sums([ov[q] for q in range(4)], u.astype(F32))
    sums = sums[:, :COLS] + sums[:, COLS:]
    sums = jnp.concatenate([sums, jnp.zeros((4, COLS), F32)], axis=0)
    g = spread(sums)
    zero = jnp.zeros_like(g)
    send_all(
        msg,
        keep[at(yh, ROWS), at(c, COLS)],
        jnp.where(yh == 0, g, zero),
        jnp.where(yh == 0, zero, g),
    )
    for q in range(4):
        ovs[q] = ov[q, at(1 - yh, ROWS), :]


def main_body(s, fit, v1, v2, o1, o2, u, keep, send, part, full, zs, gs):
    c, yh = s[0], s[1]
    g = jnp.zeros((GROWS, COLS), F32)
    for p in range(16):
        full[p * ROWS : (p + 1) * ROWS, :] = u[p, :ROWS, :]
        g = g + u[p, ROWS:, :].astype(F32)
    gs[...] = g
    g = gs[:, at(yh, 128)]
    g = g + pltpu.roll(g, 1, 1)
    own = [jnp.full((1, 128), SCALE * fit[q], F32) for q in range(4)]
    part[...] = jnp.concatenate([*own, jnp.zeros((4, 128), F32)], axis=0) - 4.0 * g
    for k, v in enumerate((v1, v2)):
        z = jnp.dot(
            v[...].reshape(4 * 256, V), full[...], preferred_element_type=F32
        ).astype(BF)
        for q in range(4):
            zs[:, (k * 4 + q) * 256 : (k * 4 + q + 1) * 256] = z[q * 256 : (q + 1) * 256]
    a = jnp.zeros((256, COLS), F32)
    b = jnp.zeros((256, COLS), F32)
    for k, o in enumerate((o1, o2)):
        for q in range(4):
            zq = zs[:, (k * 4 + q) * 256 : (k * 4 + q + 1) * 256]
            a += jnp.dot(zq, o[q, at(c, 256), at(c, COLS)], preferred_element_type=F32)
            b += jnp.dot(
                zq, o[q, at(c, 256), at(1 - c, COLS)], preferred_element_type=F32
            )
    keep[...] = a
    send[...] = b


def pair_body(s, keep, got, part, partsw, ov, ov2, mine, other, tot):
    c, yh = s[0], s[1]
    w = part[...] + jnp.concatenate([partsw[4:8, :], partsw[0:4, :]], axis=0)
    for h in range(2):
        lanes = slice(h * 128, (h + 1) * 128)
        acc = keep[:, lanes] + got[:, lanes]
        for q in range(8):
            ref = (ov, ov2)[q // 4]
            acc += ref[q % 4, :, at(c * 2 + h, 128)].astype(F32) * w[q : q + 1, :]
        tot[:, lanes] = acc
    mine[...] = tot[at(yh, ROWS), :]
    other[...] = tot[at(1 - yh, ROWS), :].astype(BF)


def rows_body(mine, recv, total, out):
    t = mine[...] + recv[...].astype(F32)
    total[...] = t
    out[...] = t.astype(BF)


def near_body(total, before, after, three, three_half, two_half):
    two = total[...] + after[...].astype(F32)
    t = two + before[...].astype(F32)
    three[...] = t
    three_half[...] = t.astype(BF)
    two_half[...] = two.astype(BF)


def wide_body(mine, recv, out):
    total = (mine[...] + recv[...].astype(F32)).astype(BF)
    for p in range(8):
        out[p] = total


def update_body(s, three, before, after, rq, dq, ov, ov2, oth, oth2, msg):
    c, yh = s[0], s[1]
    share = three[...] + before[...].astype(F32) + after[...].astype(F32)
    u = ((rq[...] + share) / dq[...]).astype(BF)
    wide = u.astype(F32)
    rows, cols = at(yh, ROWS), at(c, COLS)
    own = spread(lane_sums([r[q, rows, cols] for r in (ov, ov2) for q in range(4)], wide))
    far = spread(lane_sums([r[q, :, cols] for r in (oth, oth2) for q in range(4)], wide))
    send_all(
        msg, u, jnp.where(yh == 0, own, far), jnp.where(yh == 0, far, own)
    )


def last_body(zm, rq, dq, out):
    share = zm[0].astype(F32)
    for p in range(1, 8):
        share += zm[p].astype(F32)
    out[...] = (rq[...] + share) / dq[...]


def join_body(s, w, wy, wc, wyc, out):
    c, yh = s[0], s[1]
    out[at(yh, ROWS), at(c, COLS)] = w[...]
    out[at(1 - yh, ROWS), at(c, COLS)] = wy[...]
    out[at(yh, ROWS), at(1 - c, COLS)] = wc[...]
    out[at(1 - yh, ROWS), at(1 - c, COLS)] = wyc[...]


def swap(value, axis):
    return lax.ppermute(value, axis, [(0, 1), (1, 0)])


def along_z(value, shift):
    n = lax.axis_size("z")
    return lax.ppermute(value, "z", [(i, (i + shift) % n) for i in range(n)])


def local(b_ov, b_vv, b_oo, rhs, fit_pert, eps_vir, eps_occ):
    s = jnp.stack([lax.axis_index("c"), lax.axis_index("yh")]).astype(jnp.int32)
    tile = sds(ROWS, COLS)
    half = sds(ROWS, COLS, dtype=BF)
    message = sds(16, PIECE, COLS, dtype=BF)
    msg, ovs, rq, dq = kernel(
        start_body,
        "start",
        [message, sds(4, ROWS, O, dtype=BF), tile, tile],
        [pltpu.VMEM((256, O), BF), pltpu.VMEM((256, O), F32)],
    )(s, rhs, eps_vir[None, :], eps_occ[None, :], b_ov)
    vv2, oo2, ov2 = swap(b_vv, "c"), swap(b_oo, "c"), swap(b_ov, "c")
    oth = oth2 = None
    for step in range(ITERS):
        msg = lax.all_to_all(msg, PLANE, 0, 0, tiled=True)
        keep, send, part = kernel(
            main_body,
            "main",
            [sds(256, COLS), sds(256, COLS), sds(8, 128)],
            [
                pltpu.VMEM((V, COLS), BF),
                pltpu.VMEM((256, V), BF),
                pltpu.VMEM((GROWS, COLS), F32),
            ],
            limit=12,
            flops=2 * 8 * 256 * 256 * (V + O),
            scalars=2,
        )(s, fit_pert, b_vv, vv2, b_oo, oo2, msg)
        mine, other = kernel(
            pair_body, "pair", [tile, half], [pltpu.VMEM((256, COLS), F32)]
        )(s, keep, swap(send, "c"), part, swap(part, "c"), b_ov, ov2)
        recv = swap(other, "yh")
        if step == ITERS - 1:
            break
        if oth is None:
            oth = swap(ovs, "yh")
            oth2 = swap(oth, "c")
        total, out = kernel(rows_body, "rows", [tile, half], scalars=0)(mine, recv)
        three, three_half, two_half = kernel(
            near_body, "near", [tile, half, half], scalars=0
        )(total, along_z(out, 1), along_z(out, -1))
        (msg,) = kernel(update_body, "update", [message])(
            s,
            three,
            along_z(two_half, 3),
            along_z(three_half, -3),
            rq,
            dq,
            b_ov,
            ov2,
            oth,
            oth2,
        )
    (zm,) = kernel(wide_body, "wide", [sds(8, ROWS, COLS, dtype=BF)], scalars=0)(
        mine, recv
    )
    zm = lax.all_to_all(zm, "z", 0, 0, tiled=True)
    (w,) = kernel(last_body, "last", [tile], scalars=0)(zm, rq, dq)
    wy, wc = swap(w, "yh"), swap(w, "c")
    return kernel(join_body, "join", [sds(256, O)])(s, w, wy, wc, swap(wy, "c"))[0]


def solution(mesh):
    split = Mesh(mesh.devices.reshape(2, 8, 2, 4, 2), ("yh", "z", "c", "x", "yl"))
    placed = (
        P(AUX, VIR, None),
        P(AUX, VIR, None),
        P(AUX, None, None),
        P(VIR, None),
        P(AUX),
        P(VIR),
        P(),
    )
    return jax.shard_map(
        local, mesh=split, in_specs=placed, out_specs=P(VIR, None), check_vma=False
    )
```

```python
import math

import jax
import jax.numpy as jnp
from jax import lax
from jax.experimental import pallas as pl
from jax.experimental.pallas import tpu as pltpu
from jax.sharding import Mesh
from jax.sharding import PartitionSpec as P

V = 2048
O = 512
NAUX = 128
ITERS = 3
AUX = ("yh", "z", "c")
VIR = ("x", "yl")
PLANE = ("x", "yl", "yh")
SCALE = math.sqrt(4.0 * V * O / NAUX)
BF, F32 = jnp.bfloat16, jnp.float32
ROWS, COLS, GROWS = 128, 256, 8
PIECE = ROWS + GROWS


def sds(*shape, dtype=F32):
    return jax.ShapeDtypeStruct(shape, dtype)


def kernel(body, name, outputs, scratch=(), limit=8, flops=0, scalars=1, far=(), out=()):
    def call(*args):
        moved = sum(math.prod(a.shape) * a.dtype.itemsize for a in (*args, *outputs))
        return pl.pallas_call(
            body,
            out_shape=list(outputs),
            in_specs=[
                pl.BlockSpec(
                    memory_space=pltpu.SMEM
                    if k < scalars
                    else pltpu.HBM
                    if k in far
                    else pltpu.VMEM
                )
                for k in range(len(args))
            ],
            out_specs=[
                pl.BlockSpec(memory_space=pltpu.HBM if k in out else pltpu.VMEM)
                for k in range(len(outputs))
            ],
            scratch_shapes=list(scratch),
            compiler_params=pltpu.CompilerParams(vmem_limit_bytes=limit << 20),
            cost_estimate=pl.CostEstimate(
                flops=flops, bytes_accessed=moved, transcendentals=0
            ),
            name=name,
        )(*args)

    return call


def at(index, size):
    return pl.ds(pl.multiple_of(index * size, size), size)


def spread(sums):
    g = jnp.sum(sums, axis=1, keepdims=True)
    high = g.astype(BF)
    low = (g - high.astype(F32)).astype(BF)
    lane = lax.broadcasted_iota(jnp.int32, (GROWS, 128), 1)
    wide = (GROWS, 128)
    return jnp.where(
        lane % 2 == 0,
        jnp.broadcast_to(high.astype(F32), wide),
        jnp.broadcast_to(low.astype(F32), wide),
    )


def send_all(msg, body, left, right):
    block = jnp.concatenate([left, right], axis=1).astype(BF)
    for p in range(16):
        msg[p, :ROWS, :] = body
        msg[p, ROWS:, :] = block


def lane_sums(refs, wide):
    return jnp.concatenate(
        [jnp.sum(v.astype(F32) * wide, axis=0, keepdims=True) for v in refs], axis=0
    )


def start_body(
    s, rhs_h, ev_h, eo_h, ov_h, msg_h, rq, dq, rhs, ev, eo, ov, msg, keep, den, sems
):
    c, yh = s[0], s[1]
    copies = [
        pltpu.make_async_copy(src, dst, sems.at[k])
        for k, (src, dst) in enumerate(
            ((ev_h, ev), (eo_h, eo), (rhs_h, rhs), (ov_h, ov))
        )
    ]
    for copy in copies:
        copy.start()
    copies[0].wait()
    copies[1].wait()
    column = jnp.broadcast_to(ev[...], (128, 256)).T
    for h in range(4):
        lanes = slice(h * 128, (h + 1) * 128)
        den[:, lanes] = column - eo[:, lanes]
    copies[2].wait()
    u = (rhs[...] / den[...]).astype(BF)
    keep[...] = u
    rq[...] = rhs[at(yh, ROWS), at(c, COLS)]
    dq[...] = den[at(yh, ROWS), at(c, COLS)]
    copies[3].wait()
    sums = lane_sums([ov[q] for q in range(4)], u.astype(F32))
    sums = sums[:, :COLS] + sums[:, COLS:]
    sums = jnp.concatenate([sums, jnp.zeros((4, COLS), F32)], axis=0)
    g = spread(sums)
    zero = jnp.zeros_like(g)
    send_all(
        msg,
        keep[at(yh, ROWS), at(c, COLS)],
        jnp.where(yh == 0, g, zero),
        jnp.where(yh == 0, zero, g),
    )
    out = pltpu.make_async_copy(msg, msg_h, sems.at[4])
    out.start()
    out.wait()


def main_body(
    s, fit, v1_h, v2_h, o1_h, o2_h, u, keep, send, part, v, o, full, zs, gs, sems
):
    c, yh = s[0], s[1]
    pieces = ((v1_h, 0, 1), (v1_h, 1, 4), (v2_h, 0, 4))
    copies = []
    for k, (src, low, high) in enumerate(pieces):
        dst = v.at[pl.ds(low + (4 if src is v2_h else 0), high - low)]
        copies.append(
            pltpu.make_async_copy(src.at[pl.ds(low, high - low)], dst, sems.at[k])
        )
    for k, src in enumerate((o1_h, o2_h)):
        copies.append(
            pltpu.make_async_copy(
                src.at[:, at(c, 256), :], o.at[pl.ds(4 * k, 4)], sems.at[3 + k]
            )
        )
    for copy in copies:
        copy.start()
    g = jnp.zeros((GROWS, COLS), F32)
    for p in range(16):
        full[p * ROWS : (p + 1) * ROWS, :] = u[p, :ROWS, :]
        g = g + u[p, ROWS:, :].astype(F32)
    gs[...] = g
    g = gs[:, at(yh, 128)]
    g = g + pltpu.roll(g, 1, 1)
    own = [jnp.full((1, 128), SCALE * fit[q], F32) for q in range(4)]
    part[...] = jnp.concatenate([*own, jnp.zeros((4, 128), F32)], axis=0) - 4.0 * g
    for k, (low, high) in enumerate(((0, 1), (1, 4), (4, 8))):
        copies[k].wait()
        z = jnp.dot(
            v[low:high].reshape((high - low) * 256, V),
            full[...],
            preferred_element_type=F32,
        ).astype(BF)
        for q in range(low, high):
            zs[:, q * 256 : (q + 1) * 256] = z[(q - low) * 256 : (q - low + 1) * 256]
    copies[3].wait()
    copies[4].wait()
    a = jnp.zeros((256, COLS), F32)
    b = jnp.zeros((256, COLS), F32)
    for q in range(8):
        zq = zs[:, q * 256 : (q + 1) * 256]
        a += jnp.dot(zq, o[q, :, at(c, COLS)], preferred_element_type=F32)
        b += jnp.dot(zq, o[q, :, at(1 - c, COLS)], preferred_element_type=F32)
    keep[...] = a
    send[...] = b


def pair_body(s, keep, got, part, partsw, ov, ov2, mine, other, tot):
    c, yh = s[0], s[1]
    w = part[...] + jnp.concatenate([partsw[4:8, :], partsw[0:4, :]], axis=0)
    for h in range(2):
        lanes = slice(h * 128, (h + 1) * 128)
        acc = keep[:, lanes] + got[:, lanes]
        for q in range(8):
            ref = (ov, ov2)[q // 4]
            acc += ref[q % 4, :, at(c * 2 + h, 128)].astype(F32) * w[q : q + 1, :]
        tot[:, lanes] = acc
    mine[...] = tot[at(yh, ROWS), :]
    other[...] = tot[at(1 - yh, ROWS), :].astype(BF)


def rows_body(mine, recv, total, out):
    t = mine[...] + recv[...].astype(F32)
    total[...] = t
    out[...] = t.astype(BF)


def first_rows_body(s, mine, recv, ov, ov2, total, out, ovs):
    c, yh = s[0], s[1]
    rows_body(mine, recv, total, out)
    for q in range(8):
        ovs[q] = (ov, ov2)[q // 4][q % 4, at(1 - yh, ROWS), at(c, COLS)]


def near_body(total, before, after, three, three_half, two_half):
    two = total[...] + after[...].astype(F32)
    t = two + before[...].astype(F32)
    three[...] = t
    three_half[...] = t.astype(BF)
    two_half[...] = two.astype(BF)


def wide_body(mine, recv, out):
    total = (mine[...] + recv[...].astype(F32)).astype(BF)
    for p in range(8):
        out[p] = total


def update_body(s, three, before, after, rq, dq, ov, ov2, oth, msg):
    c, yh = s[0], s[1]
    share = three[...] + before[...].astype(F32) + after[...].astype(F32)
    u = ((rq[...] + share) / dq[...]).astype(BF)
    wide = u.astype(F32)
    rows, cols = at(yh, ROWS), at(c, COLS)
    own = spread(lane_sums([r[q, rows, cols] for r in (ov, ov2) for q in range(4)], wide))
    far = spread(lane_sums([oth[q] for q in range(8)], wide))
    send_all(
        msg, u, jnp.where(yh == 0, own, far), jnp.where(yh == 0, far, own)
    )


def last_body(zm, rq, dq, out):
    share = zm[0].astype(F32)
    for p in range(1, 8):
        share += zm[p].astype(F32)
    out[...] = (rq[...] + share) / dq[...]


def join_body(s, w, wy, wc, wyc, out):
    c, yh = s[0], s[1]
    out[at(yh, ROWS), at(c, COLS)] = w[...]
    out[at(1 - yh, ROWS), at(c, COLS)] = wy[...]
    out[at(yh, ROWS), at(1 - c, COLS)] = wc[...]
    out[at(1 - yh, ROWS), at(1 - c, COLS)] = wyc[...]


def swap(value, axis):
    return lax.ppermute(value, axis, [(0, 1), (1, 0)])


def along_z(value, shift):
    n = lax.axis_size("z")
    return lax.ppermute(value, "z", [(i, (i + shift) % n) for i in range(n)])


def local(b_ov, b_vv, b_oo, rhs, fit_pert, eps_vir, eps_occ):
    s = jnp.stack([lax.axis_index("c"), lax.axis_index("yh")]).astype(jnp.int32)
    tile = sds(ROWS, COLS)
    half = sds(ROWS, COLS, dtype=BF)
    message = sds(16, PIECE, COLS, dtype=BF)
    msg, rq, dq = kernel(
        start_body,
        "start",
        [message, tile, tile],
        [
            pltpu.VMEM((256, O), F32),
            pltpu.VMEM((1, 256), F32),
            pltpu.VMEM((1, O), F32),
            pltpu.VMEM((4, 256, O), BF),
            pltpu.VMEM((16, PIECE, COLS), BF),
            pltpu.VMEM((256, O), BF),
            pltpu.VMEM((256, O), F32),
            pltpu.SemaphoreType.DMA((5,)),
        ],
        limit=60,
        far=range(1, 5),
        out=(0,),
    )(s, rhs, eps_vir[None, :], eps_occ[None, :], b_ov)
    vv2, oo2, ov2 = swap(b_vv, "c"), swap(b_oo, "c"), swap(b_ov, "c")
    oth = None
    for step in range(ITERS):
        msg = lax.all_to_all(msg, PLANE, 0, 0, tiled=True)
        keep, send, part = kernel(
            main_body,
            "main",
            [sds(256, COLS), sds(256, COLS), sds(8, 128)],
            [
                pltpu.VMEM((8, 256, V), BF),
                pltpu.VMEM((8, 256, O), BF),
                pltpu.VMEM((V, COLS), BF),
                pltpu.VMEM((256, V), BF),
                pltpu.VMEM((GROWS, COLS), F32),
                pltpu.SemaphoreType.DMA((5,)),
            ],
            limit=52,
            far=range(2, 6),
            flops=2 * 8 * 256 * 256 * (V + O),
            scalars=2,
        )(s, fit_pert, b_vv, vv2, b_oo, oo2, msg)
        mine, other = kernel(
            pair_body, "pair", [tile, half], [pltpu.VMEM((256, COLS), F32)]
        )(s, keep, swap(send, "c"), part, swap(part, "c"), b_ov, ov2)
        recv = swap(other, "yh")
        if step == ITERS - 1:
            break
        if oth is None:
            total, out, ovs = kernel(
                first_rows_body,
                "first_rows",
                [tile, half, sds(8, ROWS, COLS, dtype=BF)],
            )(s, mine, recv, b_ov, ov2)
            oth = swap(ovs, "yh")
        else:
            total, out = kernel(rows_body, "rows", [tile, half], scalars=0)(mine, recv)
        three, three_half, two_half = kernel(
            near_body, "near", [tile, half, half], scalars=0
        )(total, along_z(out, 1), along_z(out, -1))
        (msg,) = kernel(update_body, "update", [message])(
            s,
            three,
            along_z(two_half, 3),
            along_z(three_half, -3),
            rq,
            dq,
            b_ov,
            ov2,
            oth,
        )
    (zm,) = kernel(wide_body, "wide", [sds(8, ROWS, COLS, dtype=BF)], scalars=0)(
        mine, recv
    )
    zm = lax.all_to_all(zm, "z", 0, 0, tiled=True)
    (w,) = kernel(last_body, "last", [tile], scalars=0)(zm, rq, dq)
    wy, wc = swap(w, "yh"), swap(w, "c")
    return kernel(join_body, "join", [sds(256, O)])(s, w, wy, wc, swap(wy, "c"))[0]


def solution(mesh):
    split = Mesh(mesh.devices.reshape(2, 8, 2, 4, 2), ("yh", "z", "c", "x", "yl"))
    placed = (
        P(AUX, VIR, None),
        P(AUX, VIR, None),
        P(AUX, None, None),
        P(VIR, None),
        P(AUX),
        P(VIR),
        P(),
    )
    return jax.shard_map(
        local, mesh=split, in_specs=placed, out_specs=P(VIR, None), check_vma=False
    )
```

```python
import math

import jax
import jax.numpy as jnp
from jax import lax
from jax.experimental import pallas as pl
from jax.experimental.pallas import tpu as pltpu
from jax.sharding import Mesh
from jax.sharding import PartitionSpec as P

V = 2048
O = 512
NAUX = 128
ITERS = 3
AUX = ("yh", "z", "c")
VIR = ("x", "yl")
PLANE = ("x", "yl", "yh")
SCALE = math.sqrt(4.0 * V * O / NAUX)
BF, F32 = jnp.bfloat16, jnp.float32
ROWS, COLS, GROWS = 128, 256, 8
PIECE = ROWS + GROWS


def sds(*shape, dtype=F32):
    return jax.ShapeDtypeStruct(shape, dtype)


def kernel(body, name, outputs, scratch=(), limit=8, flops=0, scalars=1, far=(), out=()):
    def call(*args):
        moved = sum(math.prod(a.shape) * jnp.dtype(a.dtype).itemsize for a in (*args, *outputs))
        return pl.pallas_call(
            body,
            out_shape=list(outputs),
            in_specs=[
                pl.BlockSpec(
                    memory_space=pltpu.SMEM
                    if k < scalars
                    else pltpu.HBM
                    if k in far
                    else pltpu.VMEM
                )
                for k in range(len(args))
            ],
            out_specs=[
                pl.BlockSpec(memory_space=pltpu.HBM if k in out else pltpu.VMEM)
                for k in range(len(outputs))
            ],
            scratch_shapes=list(scratch),
            compiler_params=pltpu.CompilerParams(vmem_limit_bytes=limit << 20),
            cost_estimate=pl.CostEstimate(
                flops=flops, bytes_accessed=moved, transcendentals=0
            ),
            name=name,
        )(*args)

    return call


def at(index, size):
    return pl.ds(pl.multiple_of(index * size, size), size)


def spread(sums):
    g = jnp.sum(sums, axis=1, keepdims=True)
    high = g.astype(BF)
    low = (g - high.astype(F32)).astype(BF)
    lane = lax.broadcasted_iota(jnp.int32, (GROWS, 128), 1)
    wide = (GROWS, 128)
    return jnp.where(
        lane % 2 == 0,
        jnp.broadcast_to(high.astype(F32), wide),
        jnp.broadcast_to(low.astype(F32), wide),
    )


def send_all(msg, body, left, right):
    block = jnp.concatenate([left, right], axis=1).astype(BF)
    for p in range(16):
        msg[p, :ROWS, :] = body
        msg[p, ROWS:, :] = block


def lane_sums(refs, wide):
    return jnp.concatenate(
        [jnp.sum(v.astype(F32) * wide, axis=0, keepdims=True) for v in refs], axis=0
    )


def start_body(
    s, rhs_h, ev_h, eo_h, ov_h, msg, rq, dq, rhs, ev, eo, ov, keep, den, sems
):
    c, yh = s[0], s[1]
    copies = [
        pltpu.make_async_copy(src, dst, sems.at[k])
        for k, (src, dst) in enumerate(
            ((ev_h, ev), (eo_h, eo), (rhs_h, rhs), (ov_h, ov))
        )
    ]
    for copy in copies:
        copy.start()
    copies[0].wait()
    copies[1].wait()
    column = jnp.broadcast_to(ev[...], (128, 256)).T
    for h in range(4):
        lanes = slice(h * 128, (h + 1) * 128)
        den[:, lanes] = column - eo[:, lanes]
    copies[2].wait()
    u = (rhs[...] / den[...]).astype(BF)
    keep[...] = u
    rq[...] = rhs[at(yh, ROWS), at(c, COLS)]
    dq[...] = den[at(yh, ROWS), at(c, COLS)]
    copies[3].wait()
    sums = lane_sums([ov[q] for q in range(4)], u.astype(F32))
    sums = sums[:, :COLS] + sums[:, COLS:]
    sums = jnp.concatenate([sums, jnp.zeros((4, COLS), F32)], axis=0)
    g = spread(sums)
    zero = jnp.zeros_like(g)
    send_all(
        msg,
        keep[at(yh, ROWS), at(c, COLS)],
        jnp.where(yh == 0, g, zero),
        jnp.where(yh == 0, zero, g),
    )


def load_body(s, v1, v2, after, v, sems):
    copies = [
        pltpu.make_async_copy(src.at[q], v.at[4 * k + q], sems.at[4 * k + q])
        for k, src in enumerate((v1, v2))
        for q in range(4)
    ]
    for copy in copies:
        copy.start()
    for copy in copies:
        copy.wait()


def main_body(s, fit, v, o1, o2, u, keep, send, part, full, zs, gs, ac):
    c, yh = s[0], s[1]
    g = jnp.zeros((GROWS, COLS), F32)
    for p in range(16):
        full[p * ROWS : (p + 1) * ROWS, :] = u[p, :ROWS, :]
        g = g + u[p, ROWS:, :].astype(F32)
    gs[...] = g
    g = gs[:, at(yh, 128)]
    g = g + pltpu.roll(g, 1, 1)
    own = [jnp.full((1, 128), SCALE * fit[q], F32) for q in range(4)]
    part[...] = jnp.concatenate([*own, jnp.zeros((4, 128), F32)], axis=0) - 4.0 * g
    for k in range(2):
        z = jnp.dot(
            v[4 * k : 4 * k + 4].reshape(4 * 256, V),
            full[...],
            preferred_element_type=F32,
        ).astype(BF)
        for q in range(4):
            zs[:, (k * 4 + q) * 256 : (k * 4 + q + 1) * 256] = z[q * 256 : (q + 1) * 256]
    o = jnp.concatenate([r[q, at(c, 256), :] for r in (o1, o2) for q in range(4)], axis=0)
    ac[...] = jnp.dot(zs[...], o, preferred_element_type=F32)
    keep[...] = ac[:, at(c, COLS)]
    send[...] = ac[:, at(1 - c, COLS)]


def pair_body(s, keep, got, part, partsw, ov, ov2, mine, other, tot):
    c, yh = s[0], s[1]
    w = part[...] + jnp.concatenate([partsw[4:8, :], partsw[0:4, :]], axis=0)
    for h in range(2):
        lanes = slice(h * 128, (h + 1) * 128)
        acc = keep[:, lanes] + got[:, lanes]
        for q in range(8):
            ref = (ov, ov2)[q // 4]
            acc += ref[q % 4, :, at(c * 2 + h, 128)].astype(F32) * w[q : q + 1, :]
        tot[:, lanes] = acc
    mine[...] = tot[at(yh, ROWS), :]
    other[...] = tot[at(1 - yh, ROWS), :].astype(BF)


def rows_body(mine, recv, total, out):
    t = mine[...] + recv[...].astype(F32)
    total[...] = t
    out[...] = t.astype(BF)


def first_rows_body(s, mine, recv, ov, ov2, total, out, ovs):
    c, yh = s[0], s[1]
    rows_body(mine, recv, total, out)
    for q in range(8):
        ovs[q] = (ov, ov2)[q // 4][q % 4, at(1 - yh, ROWS), at(c, COLS)]


def near_body(total, before, after, three, three_half, two_half):
    two = total[...] + after[...].astype(F32)
    t = two + before[...].astype(F32)
    three[...] = t
    three_half[...] = t.astype(BF)
    two_half[...] = two.astype(BF)


def wide_body(mine, recv, out):
    total = (mine[...] + recv[...].astype(F32)).astype(BF)
    for p in range(8):
        out[p] = total


def update_body(s, three, before, after, rq, dq, ov, ov2, oth, msg):
    c, yh = s[0], s[1]
    share = three[...] + before[...].astype(F32) + after[...].astype(F32)
    u = ((rq[...] + share) / dq[...]).astype(BF)
    wide = u.astype(F32)
    rows, cols = at(yh, ROWS), at(c, COLS)
    own = spread(lane_sums([r[q, rows, cols] for r in (ov, ov2) for q in range(4)], wide))
    far = spread(lane_sums([oth[q] for q in range(8)], wide))
    send_all(
        msg, u, jnp.where(yh == 0, own, far), jnp.where(yh == 0, far, own)
    )


def last_body(zm, rq, dq, out):
    share = zm[0].astype(F32)
    for p in range(1, 8):
        share += zm[p].astype(F32)
    out[...] = (rq[...] + share) / dq[...]


def join_body(s, w, wy, wc, wyc, out):
    c, yh = s[0], s[1]
    out[at(yh, ROWS), at(c, COLS)] = w[...]
    out[at(1 - yh, ROWS), at(c, COLS)] = wy[...]
    out[at(yh, ROWS), at(1 - c, COLS)] = wc[...]
    out[at(1 - yh, ROWS), at(1 - c, COLS)] = wyc[...]


def swap(value, axis):
    return lax.ppermute(value, axis, [(0, 1), (1, 0)])


def along_z(value, shift):
    n = lax.axis_size("z")
    return lax.ppermute(value, "z", [(i, (i + shift) % n) for i in range(n)])


def local(b_ov, b_vv, b_oo, rhs, fit_pert, eps_vir, eps_occ):
    s = jnp.stack([lax.axis_index("c"), lax.axis_index("yh")]).astype(jnp.int32)
    tile = sds(ROWS, COLS)
    half = sds(ROWS, COLS, dtype=BF)
    message = sds(16, PIECE, COLS, dtype=BF)
    msg, rq, dq = kernel(
        start_body,
        "start",
        [message, tile, tile],
        [
            pltpu.VMEM((256, O), F32),
            pltpu.VMEM((1, 256), F32),
            pltpu.VMEM((1, O), F32),
            pltpu.VMEM((4, 256, O), BF),
            pltpu.VMEM((256, O), BF),
            pltpu.VMEM((256, O), F32),
            pltpu.SemaphoreType.DMA((5,)),
        ],
        limit=12,
        far=range(1, 5),
    )(
        s,
        *(
            pltpu.with_memory_space_constraint(a, pltpu.HBM)
            for a in (rhs, eps_vir[None, :], eps_occ[None, :], b_ov)
        ),
    )
    vv2, oo2 = swap(b_vv, "c"), swap(b_oo, "c")
    oth = None
    for step in range(ITERS):
        msg = lax.all_to_all(msg, PLANE, 0, 0, tiled=True)
        if oth is None:
            msg, b_ov, fit_pert, s = lax.optimization_barrier((msg, b_ov, fit_pert, s))
            ov2 = swap(b_ov, "c")
            (vv,) = kernel(
                load_body,
                "load",
                [pltpu.VMEM((8, 256, V), BF)],
                [pltpu.SemaphoreType.DMA((8,))],
                far=(1, 2),
            )(
                s,
                *(
                    pltpu.with_memory_space_constraint(a, pltpu.HBM)
                    for a in (b_vv, vv2)
                ),
                msg[:1, :8, :128],
            )
        keep, send, part = kernel(
            main_body,
            "main",
            [sds(256, COLS), sds(256, COLS), sds(8, 128)],
            [
                pltpu.VMEM((V, COLS), BF),
                pltpu.VMEM((256, V), BF),
                pltpu.VMEM((GROWS, COLS), F32),
                pltpu.VMEM((256, O), F32),
            ],
            limit=12,
            flops=2 * 8 * 256 * 256 * (V + O),
            scalars=2,
        )(s, fit_pert, vv, b_oo, oo2, msg)
        mine, other = kernel(
            pair_body, "pair", [tile, half], [pltpu.VMEM((256, COLS), F32)]
        )(s, keep, swap(send, "c"), part, swap(part, "c"), b_ov, ov2)
        recv = swap(other, "yh")
        if step == ITERS - 1:
            break
        if oth is None:
            total, out, ovs = kernel(
                first_rows_body,
                "first_rows",
                [tile, half, sds(8, ROWS, COLS, dtype=BF)],
            )(s, mine, recv, b_ov, ov2)
            oth = swap(ovs, "yh")
        else:
            total, out = kernel(rows_body, "rows", [tile, half], scalars=0)(mine, recv)
        three, three_half, two_half = kernel(
            near_body, "near", [tile, half, half], scalars=0
        )(total, along_z(out, 1), along_z(out, -1))
        (msg,) = kernel(update_body, "update", [message])(
            s,
            three,
            along_z(two_half, 3),
            along_z(three_half, -3),
            rq,
            dq,
            b_ov,
            ov2,
            oth,
        )
    (zm,) = kernel(wide_body, "wide", [sds(8, ROWS, COLS, dtype=BF)], scalars=0)(
        mine, recv
    )
    zm = lax.all_to_all(zm, "z", 0, 0, tiled=True)
    (w,) = kernel(last_body, "last", [tile], scalars=0)(zm, rq, dq)
    wy, wc = swap(w, "yh"), swap(w, "c")
    return kernel(join_body, "join", [sds(256, O)])(s, w, wy, wc, swap(wy, "c"))[0]


def solution(mesh):
    split = Mesh(mesh.devices.reshape(2, 8, 2, 4, 2), ("yh", "z", "c", "x", "yl"))
    placed = (
        P(AUX, VIR, None),
        P(AUX, VIR, None),
        P(AUX, None, None),
        P(VIR, None),
        P(AUX),
        P(VIR),
        P(),
    )
    return jax.shard_map(
        local, mesh=split, in_specs=placed, out_specs=P(VIR, None), check_vma=False
    )
```

```python
import math

import jax
import jax.numpy as jnp
from jax import lax
from jax.experimental import pallas as pl
from jax.experimental.pallas import tpu as pltpu
from jax.sharding import Mesh
from jax.sharding import PartitionSpec as P

V = 2048
O = 512
NAUX = 128
ITERS = 3
AUX = ("yh", "z", "c")
VIR = ("x", "yl")
PLANE = ("x", "yl", "yh")
SCALE = math.sqrt(4.0 * V * O / NAUX)
BF, F32 = jnp.bfloat16, jnp.float32
ROWS, COLS, GROWS = 128, 256, 8
PIECE = ROWS + GROWS


def sds(*shape, dtype=F32):
    return jax.ShapeDtypeStruct(shape, dtype)


def kernel(body, name, outputs, scratch=(), limit=8, flops=0, scalars=1, far=(), out=()):
    def call(*args):
        moved = sum(math.prod(a.shape) * jnp.dtype(a.dtype).itemsize for a in (*args, *outputs))
        return pl.pallas_call(
            body,
            out_shape=list(outputs),
            in_specs=[
                pl.BlockSpec(
                    memory_space=pltpu.SMEM
                    if k < scalars
                    else pltpu.HBM
                    if k in far
                    else pltpu.VMEM
                )
                for k in range(len(args))
            ],
            out_specs=[
                pl.BlockSpec(memory_space=pltpu.HBM if k in out else pltpu.VMEM)
                for k in range(len(outputs))
            ],
            scratch_shapes=list(scratch),
            compiler_params=pltpu.CompilerParams(vmem_limit_bytes=limit << 20),
            cost_estimate=pl.CostEstimate(
                flops=flops, bytes_accessed=moved, transcendentals=0
            ),
            name=name,
        )(*args)

    return call


def at(index, size):
    return pl.ds(pl.multiple_of(index * size, size), size)


def spread(sums):
    g = jnp.sum(sums, axis=1, keepdims=True)
    high = g.astype(BF)
    low = (g - high.astype(F32)).astype(BF)
    lane = lax.broadcasted_iota(jnp.int32, (GROWS, 128), 1)
    wide = (GROWS, 128)
    return jnp.where(
        lane % 2 == 0,
        jnp.broadcast_to(high.astype(F32), wide),
        jnp.broadcast_to(low.astype(F32), wide),
    )


def send_all(msg, body, left, right):
    block = jnp.concatenate([left, right], axis=1).astype(BF)
    for p in range(16):
        msg[p, :ROWS, :] = body
        msg[p, ROWS:, :] = block


def lane_sums(refs, wide):
    return jnp.concatenate(
        [jnp.sum(v.astype(F32) * wide, axis=0, keepdims=True) for v in refs], axis=0
    )


def start_body(
    s, rhs_h, ev_h, eo_h, ov_h, v_h, msg, rq, dq, v, rhs, ev, eo, ov, keep, den, sems
):
    c, yh = s[0], s[1]
    copies = [
        pltpu.make_async_copy(src, dst, sems.at[k])
        for k, (src, dst) in enumerate(
            ((ev_h, ev), (eo_h, eo), (rhs_h, rhs), (ov_h, ov), (v_h, v))
        )
    ]
    for copy in copies:
        copy.start()
    copies[0].wait()
    copies[1].wait()
    column = jnp.broadcast_to(ev[...], (128, 256)).T
    for h in range(4):
        lanes = slice(h * 128, (h + 1) * 128)
        den[:, lanes] = column - eo[:, lanes]
    copies[2].wait()
    u = (rhs[...] / den[...]).astype(BF)
    keep[...] = u
    rq[...] = rhs[at(yh, ROWS), at(c, COLS)]
    dq[...] = den[at(yh, ROWS), at(c, COLS)]
    copies[3].wait()
    sums = lane_sums([ov[q] for q in range(4)], u.astype(F32))
    sums = sums[:, :COLS] + sums[:, COLS:]
    sums = jnp.concatenate([sums, jnp.zeros((4, COLS), F32)], axis=0)
    g = spread(sums)
    zero = jnp.zeros_like(g)
    send_all(
        msg,
        keep[at(yh, ROWS), at(c, COLS)],
        jnp.where(yh == 0, g, zero),
        jnp.where(yh == 0, zero, g),
    )
    copies[4].wait()


def load_body(s, v_h, after, v, sems):
    copies = [pltpu.make_async_copy(v_h.at[q], v.at[q], sems.at[q]) for q in range(4)]
    for copy in copies:
        copy.start()
    for copy in copies:
        copy.wait()


def main_body(s, fit, v1, v2, o1, o2, u, keep, send, part, full, zs, gs, ac):
    c, yh = s[0], s[1]
    g = jnp.zeros((GROWS, COLS), F32)
    for p in range(16):
        full[p * ROWS : (p + 1) * ROWS, :] = u[p, :ROWS, :]
        g = g + u[p, ROWS:, :].astype(F32)
    gs[...] = g
    g = gs[:, at(yh, 128)]
    g = g + pltpu.roll(g, 1, 1)
    own = [jnp.full((1, 128), SCALE * fit[q], F32) for q in range(4)]
    part[...] = jnp.concatenate([*own, jnp.zeros((4, 128), F32)], axis=0) - 4.0 * g
    for k, v in enumerate((v1, v2)):
        z = jnp.dot(
            v[...].reshape(4 * 256, V), full[...], preferred_element_type=F32
        ).astype(BF)
        for q in range(4):
            zs[:, (k * 4 + q) * 256 : (k * 4 + q + 1) * 256] = z[q * 256 : (q + 1) * 256]
    o = jnp.concatenate([r[q, at(c, 256), :] for r in (o1, o2) for q in range(4)], axis=0)
    ac[...] = jnp.dot(zs[...], o, preferred_element_type=F32)
    keep[...] = ac[:, at(c, COLS)]
    send[...] = ac[:, at(1 - c, COLS)]


def chip_total(s, keep, got, part, partsw, ov, ov2, tot):
    c = s[0]
    w = part[...] + jnp.concatenate([partsw[4:8, :], partsw[0:4, :]], axis=0)
    for h in range(2):
        lanes = slice(h * 128, (h + 1) * 128)
        acc = keep[:, lanes] + got[:, lanes]
        for q in range(8):
            ref = (ov, ov2)[q // 4]
            acc += ref[q % 4, :, at(c * 2 + h, 128)].astype(F32) * w[q : q + 1, :]
        tot[:, lanes] = acc


def pair_body(s, keep, got, part, partsw, ov, ov2, mine, other, tot):
    yh = s[1]
    chip_total(s, keep, got, part, partsw, ov, ov2, tot)
    mine[...] = tot[at(yh, ROWS), :]
    other[...] = tot[at(1 - yh, ROWS), :].astype(BF)


def rows_body(mine, recv, total, out):
    t = mine[...] + recv[...].astype(F32)
    total[...] = t
    out[...] = t.astype(BF)


def first_rows_body(s, mine, recv, ov, ov2, total, out, ovs):
    c, yh = s[0], s[1]
    rows_body(mine, recv, total, out)
    for q in range(8):
        ovs[q] = (ov, ov2)[q // 4][q % 4, at(1 - yh, ROWS), at(c, COLS)]


def near_body(total, before, after, three, three_half, two_half):
    two = total[...] + after[...].astype(F32)
    t = two + before[...].astype(F32)
    three[...] = t
    three_half[...] = t.astype(BF)
    two_half[...] = two.astype(BF)


def pieces_body(s, keep, got, part, partsw, ov, ov2, out, tot):
    chip_total(s, keep, got, part, partsw, ov, ov2, tot)
    for p in range(16):
        out[p] = tot[p * 16 : (p + 1) * 16, :].astype(BF)


def update_body(s, three, before, after, rq, dq, ov, ov2, oth, msg):
    c, yh = s[0], s[1]
    share = three[...] + before[...].astype(F32) + after[...].astype(F32)
    u = ((rq[...] + share) / dq[...]).astype(BF)
    wide = u.astype(F32)
    rows, cols = at(yh, ROWS), at(c, COLS)
    own = spread(lane_sums([r[q, rows, cols] for r in (ov, ov2) for q in range(4)], wide))
    far = spread(lane_sums([oth[q] for q in range(8)], wide))
    send_all(
        msg, u, jnp.where(yh == 0, own, far), jnp.where(yh == 0, far, own)
    )


def last_body(s, pieces, rq, dq, out):
    share = pieces[0].astype(F32)
    for p in range(1, 16):
        share += pieces[p].astype(F32)
    rows = at(s[2], 16)
    w = (rq[rows, :] + share) / dq[rows, :]
    for p in range(16):
        out[p] = w


def join_body(s, w, wc, out):
    c = s[0]
    out[:, at(c, COLS)] = w[...]
    out[:, at(1 - c, COLS)] = wc[...]


def swap(value, axis):
    return lax.ppermute(value, axis, [(0, 1), (1, 0)])


def along_z(value, shift):
    n = lax.axis_size("z")
    return lax.ppermute(value, "z", [(i, (i + shift) % n) for i in range(n)])


def local(b_ov, b_vv, b_oo, rhs, fit_pert, eps_vir, eps_occ):
    s = jnp.stack([lax.axis_index(a) for a in ("c", "yh", "z")]).astype(jnp.int32)
    tile = sds(ROWS, COLS)
    half = sds(ROWS, COLS, dtype=BF)
    message = sds(16, PIECE, COLS, dtype=BF)
    msg, rq, dq, v1 = kernel(
        start_body,
        "start",
        [message, tile, tile, pltpu.VMEM((4, 256, V), BF)],
        [
            pltpu.VMEM((256, O), F32),
            pltpu.VMEM((1, 256), F32),
            pltpu.VMEM((1, O), F32),
            pltpu.VMEM((4, 256, O), BF),
            pltpu.VMEM((256, O), BF),
            pltpu.VMEM((256, O), F32),
            pltpu.SemaphoreType.DMA((5,)),
        ],
        limit=12,
        far=range(1, 6),
    )(
        s,
        *(
            pltpu.with_memory_space_constraint(a, pltpu.HBM)
            for a in (rhs, eps_vir[None, :], eps_occ[None, :], b_ov, b_vv)
        ),
    )
    vv2, oo2 = swap(b_vv, "c"), swap(b_oo, "c")
    oth = None
    for step in range(ITERS):
        msg = lax.all_to_all(msg, PLANE, 0, 0, tiled=True)
        if oth is None:
            msg, b_ov, fit_pert, s = lax.optimization_barrier((msg, b_ov, fit_pert, s))
            ov2 = swap(b_ov, "c")
            (v2,) = kernel(
                load_body,
                "load",
                [pltpu.VMEM((4, 256, V), BF)],
                [pltpu.SemaphoreType.DMA((4,))],
                far=(1,),
            )(
                s,
                pltpu.with_memory_space_constraint(vv2, pltpu.HBM),
                msg[:1, :8, :128],
            )
        keep, send, part = kernel(
            main_body,
            "main",
            [sds(256, COLS), sds(256, COLS), sds(8, 128)],
            [
                pltpu.VMEM((V, COLS), BF),
                pltpu.VMEM((256, V), BF),
                pltpu.VMEM((GROWS, COLS), F32),
                pltpu.VMEM((256, O), F32),
            ],
            limit=12,
            flops=2 * 8 * 256 * 256 * (V + O),
            scalars=2,
        )(s, fit_pert, v1, v2, b_oo, oo2, msg)
        chip = (s, keep, swap(send, "c"), part, swap(part, "c"), b_ov, ov2)
        sums = [pltpu.VMEM((256, COLS), F32)]
        if step == ITERS - 1:
            break
        mine, other = kernel(pair_body, "pair", [tile, half], sums)(*chip)
        recv = swap(other, "yh")
        if oth is None:
            total, out, ovs = kernel(
                first_rows_body,
                "first_rows",
                [tile, half, sds(8, ROWS, COLS, dtype=BF)],
            )(s, mine, recv, b_ov, ov2)
            oth = swap(ovs, "yh")
        else:
            total, out = kernel(rows_body, "rows", [tile, half], scalars=0)(mine, recv)
        three, three_half, two_half = kernel(
            near_body, "near", [tile, half, half], scalars=0
        )(total, along_z(out, 1), along_z(out, -1))
        (msg,) = kernel(update_body, "update", [message])(
            s,
            three,
            along_z(two_half, 3),
            along_z(three_half, -3),
            rq,
            dq,
            b_ov,
            ov2,
            oth,
        )
    (pieces,) = kernel(pieces_body, "pieces", [sds(16, 16, COLS, dtype=BF)], sums)(*chip)
    pieces = lax.all_to_all(pieces, ("yh", "z"), 0, 0, tiled=True)
    (pieces,) = kernel(last_body, "last", [sds(16, 16, COLS)])(s, pieces, rq, dq)
    w = lax.all_to_all(pieces, ("yh", "z"), 0, 0, tiled=True).reshape(256, COLS)
    return kernel(join_body, "join", [sds(256, O)])(s, w, swap(w, "c"))[0]


def solution(mesh):
    split = Mesh(mesh.devices.reshape(2, 8, 2, 4, 2), ("yh", "z", "c", "x", "yl"))
    placed = (
        P(AUX, VIR, None),
        P(AUX, VIR, None),
        P(AUX, None, None),
        P(VIR, None),
        P(AUX),
        P(VIR),
        P(),
    )
    return jax.shard_map(
        local, mesh=split, in_specs=placed, out_specs=P(VIR, None), check_vma=False
    )
```

```python
import math

import jax
import jax.numpy as jnp
from jax import lax
from jax.experimental import pallas as pl
from jax.experimental.pallas import tpu as pltpu
from jax.sharding import Mesh
from jax.sharding import PartitionSpec as P


V = 2048
O = 512
NAUX = 128
ITERS = 3
AUX = ("yh", "z", "c")
VIR = ("x", "yl")
PLANE = ("x", "yl", "yh")
SCALE = math.sqrt(4.0 * V * O / NAUX)
BF, F32 = jnp.bfloat16, jnp.float32
ROWS, COLS, GROWS = 128, 256, 8
PIECE = ROWS + GROWS


def sds(*shape, dtype=F32):
    return jax.ShapeDtypeStruct(shape, dtype)


def kernel(body, outputs, scratch=(), limit=8, flops=0, scalars=1, far=(), out=()):
    def call(*args):
        moved = sum(math.prod(a.shape) * jnp.dtype(a.dtype).itemsize for a in (*args, *outputs))
        return pl.pallas_call(
            body,
            out_shape=list(outputs),
            in_specs=[
                pl.BlockSpec(
                    memory_space=pltpu.SMEM
                    if k < scalars
                    else pltpu.HBM
                    if k in far
                    else pltpu.VMEM
                )
                for k in range(len(args))
            ],
            out_specs=[
                pl.BlockSpec(memory_space=pltpu.HBM if k in out else pltpu.VMEM)
                for k in range(len(outputs))
            ],
            scratch_shapes=list(scratch),
            compiler_params=pltpu.CompilerParams(vmem_limit_bytes=limit << 20),
            cost_estimate=pl.CostEstimate(
                flops=flops, bytes_accessed=moved, transcendentals=0
            ),
        )(*args)

    return call


def at(index, size):
    return pl.ds(pl.multiple_of(index * size, size), size)


def spread(sums):
    g = jnp.sum(sums, axis=1, keepdims=True)
    high = g.astype(BF)
    low = (g - high.astype(F32)).astype(BF)
    lane = lax.broadcasted_iota(jnp.int32, (GROWS, 128), 1)
    wide = (GROWS, 128)
    return jnp.where(
        lane % 2 == 0,
        jnp.broadcast_to(high.astype(F32), wide),
        jnp.broadcast_to(low.astype(F32), wide),
    )


def send_all(msg, body, left, right):
    block = jnp.concatenate([left, right], axis=1).astype(BF)
    for p in range(16):
        msg[p, :ROWS, :] = body
        msg[p, ROWS:, :] = block


def lane_sums(refs, wide):
    return jnp.concatenate(
        [jnp.sum(v.astype(F32) * wide, axis=0, keepdims=True) for v in refs], axis=0
    )


def start_body(
    s, rhs_h, ev_h, eo_h, ov_h, v_h, msg, rq, dq, v, rhs, ev, eo, ov, keep, den, sems
):
    c, yh = s[0], s[1]
    copies = [
        pltpu.make_async_copy(src, dst, sems.at[k])
        for k, (src, dst) in enumerate(
            ((ev_h, ev), (eo_h, eo), (rhs_h, rhs), (ov_h, ov), (v_h, v))
        )
    ]
    for copy in copies:
        copy.start()
    copies[0].wait()
    copies[1].wait()
    column = jnp.broadcast_to(ev[...], (128, 256)).T
    for h in range(4):
        lanes = slice(h * 128, (h + 1) * 128)
        den[:, lanes] = column - eo[:, lanes]
    copies[2].wait()
    u = (rhs[...] / den[...]).astype(BF)
    keep[...] = u
    rq[...] = rhs[at(yh, ROWS), at(c, COLS)]
    dq[...] = den[at(yh, ROWS), at(c, COLS)]
    copies[3].wait()
    sums = lane_sums([ov[q] for q in range(4)], u.astype(F32))
    sums = sums[:, :COLS] + sums[:, COLS:]
    sums = jnp.concatenate([sums, jnp.zeros((4, COLS), F32)], axis=0)
    g = spread(sums)
    zero = jnp.zeros_like(g)
    send_all(
        msg,
        keep[at(yh, ROWS), at(c, COLS)],
        jnp.where(yh == 0, g, zero),
        jnp.where(yh == 0, zero, g),
    )
    copies[4].wait()


def load_body(s, v_h, after, v, sems):
    copies = [pltpu.make_async_copy(v_h.at[q], v.at[q], sems.at[q]) for q in range(4)]
    for copy in copies:
        copy.start()
    for copy in copies:
        copy.wait()


def main_body(s, fit, v1, v2, o1, o2, u, keep, send, part, full, zs, gs, ac):
    c, yh = s[0], s[1]
    g = jnp.zeros((GROWS, COLS), F32)
    for p in range(16):
        full[p * ROWS : (p + 1) * ROWS, :] = u[p, :ROWS, :]
        g = g + u[p, ROWS:, :].astype(F32)
    gs[...] = g
    g = gs[:, at(yh, 128)]
    g = g + pltpu.roll(g, 1, 1)
    own = [jnp.full((1, 128), SCALE * fit[q], F32) for q in range(4)]
    w = jnp.concatenate([*own, jnp.zeros((4, 128), F32)], axis=0) - 4.0 * g
    part[...] = w
    send[256:, :] = jnp.concatenate([w, w], axis=1)
    for k, v in enumerate((v1, v2)):
        z = jnp.dot(
            v[...].reshape(4 * 256, V), full[...], preferred_element_type=F32
        ).astype(BF)
        for q in range(4):
            zs[:, (k * 4 + q) * 256 : (k * 4 + q + 1) * 256] = z[q * 256 : (q + 1) * 256]
    o = jnp.concatenate([r[q, at(c, 256), :] for r in (o1, o2) for q in range(4)], axis=0)
    ac[...] = jnp.dot(zs[...], o, preferred_element_type=F32)
    keep[...] = ac[:, at(c, COLS)]
    send[:256, :] = ac[:, at(1 - c, COLS)]


def chip_total(s, keep, got, part, ov, ov2, tot):
    c = s[0]
    other = got[256:, :128]
    w = part[...] + jnp.concatenate([other[4:8, :], other[0:4, :]], axis=0)
    for h in range(2):
        lanes = slice(h * 128, (h + 1) * 128)
        acc = keep[:, lanes] + got[:256, lanes]
        for q in range(8):
            ref = (ov, ov2)[q // 4]
            acc += ref[q % 4, :, at(c * 2 + h, 128)].astype(F32) * w[q : q + 1, :]
        tot[:, lanes] = acc


def pair_body(s, keep, got, part, ov, ov2, mine, other, tot):
    yh = s[1]
    chip_total(s, keep, got, part, ov, ov2, tot)
    mine[...] = tot[at(yh, ROWS), :]
    other[...] = tot[at(1 - yh, ROWS), :].astype(BF)


def rows_body(mine, recv, total, out):
    t = mine[...] + recv[...].astype(F32)
    total[...] = t
    out[...] = t.astype(BF)


def first_pair_body(s, keep, got, part, ov, ov2, mine, other, ovs, tot):
    c, yh = s[0], s[1]
    pair_body(s, keep, got, part, ov, ov2, mine, other, tot)
    for q in range(8):
        ovs[q] = (ov, ov2)[q // 4][q % 4, at(1 - yh, ROWS), at(c, COLS)]


def near_body(total, before, after, three, three_half, two_half):
    two = total[...] + after[...].astype(F32)
    t = two + before[...].astype(F32)
    three[...] = t
    three_half[...] = t.astype(BF)
    two_half[...] = two.astype(BF)


def pieces_body(s, keep, got, part, ov, ov2, out, tot):
    chip_total(s, keep, got, part, ov, ov2, tot)
    for p in range(16):
        out[p] = tot[p * 16 : (p + 1) * 16, :].astype(BF)


def update_body(s, three, before, after, rq, dq, ov, ov2, oth, msg):
    c, yh = s[0], s[1]
    share = three[...] + before[...].astype(F32) + after[...].astype(F32)
    u = ((rq[...] + share) / dq[...]).astype(BF)
    wide = u.astype(F32)
    rows, cols = at(yh, ROWS), at(c, COLS)
    own = spread(lane_sums([r[q, rows, cols] for r in (ov, ov2) for q in range(4)], wide))
    far = spread(lane_sums([oth[q] for q in range(8)], wide))
    send_all(
        msg, u, jnp.where(yh == 0, own, far), jnp.where(yh == 0, far, own)
    )


def last_body(s, pieces, rq, dq, out):
    share = pieces[0].astype(F32)
    for p in range(1, 16):
        share += pieces[p].astype(F32)
    rows = at(s[2], 16)
    w = (rq[rows, :] + share) / dq[rows, :]
    for p in range(16):
        out[p] = w


def join_body(s, w, wc, out):
    c = s[0]
    out[:, at(c, COLS)] = w[...]
    out[:, at(1 - c, COLS)] = wc[...]


def swap(value, axis):
    return lax.ppermute(value, axis, [(0, 1), (1, 0)])


def along_z(value, shift):
    n = lax.axis_size("z")
    return lax.ppermute(value, "z", [(i, (i + shift) % n) for i in range(n)])


def local(b_ov, b_vv, b_oo, rhs, fit_pert, eps_vir, eps_occ):
    s = jnp.stack([lax.axis_index(a) for a in ("c", "yh", "z")]).astype(jnp.int32)
    tile = sds(ROWS, COLS)
    half = sds(ROWS, COLS, dtype=BF)
    message = sds(16, PIECE, COLS, dtype=BF)
    msg, rq, dq, v1 = kernel(
        start_body,
        [message, tile, tile, pltpu.VMEM((4, 256, V), BF)],
        [
            pltpu.VMEM((256, O), F32),
            pltpu.VMEM((1, 256), F32),
            pltpu.VMEM((1, O), F32),
            pltpu.VMEM((4, 256, O), BF),
            pltpu.VMEM((256, O), BF),
            pltpu.VMEM((256, O), F32),
            pltpu.SemaphoreType.DMA((5,)),
        ],
        limit=12,
        far=range(1, 6),
    )(
        s,
        *(
            pltpu.with_memory_space_constraint(a, pltpu.HBM)
            for a in (rhs, eps_vir[None, :], eps_occ[None, :], b_ov, b_vv)
        ),
    )
    vv2, oo2 = swap(b_vv, "c"), swap(b_oo, "c")
    oth = None
    for step in range(ITERS):
        msg = lax.all_to_all(msg, PLANE, 0, 0, tiled=True)
        if oth is None:
            msg, b_ov, fit_pert, s = lax.optimization_barrier((msg, b_ov, fit_pert, s))
            ov2 = swap(b_ov, "c")
            (v2,) = kernel(
                load_body, [pltpu.VMEM((4, 256, V), BF)], [pltpu.SemaphoreType.DMA((4,))], far=(1,)
            )(
                s,
                pltpu.with_memory_space_constraint(vv2, pltpu.HBM),
                msg[:1, :8, :128],
            )
        keep, send, part = kernel(
            main_body,
            [sds(256, COLS), sds(256 + 8, COLS), sds(8, 128)],
            [
                pltpu.VMEM((V, COLS), BF),
                pltpu.VMEM((256, V), BF),
                pltpu.VMEM((GROWS, COLS), F32),
                pltpu.VMEM((256, O), F32),
            ],
            limit=12,
            flops=2 * 8 * 256 * 256 * (V + O),
            scalars=2,
        )(s, fit_pert, v1, v2, b_oo, oo2, msg)
        chip = (s, keep, swap(send, "c"), part, b_ov, ov2)
        sums = [pltpu.VMEM((256, COLS), F32)]
        if step == ITERS - 1:
            break
        if oth is None:
            mine, other, ovs = kernel(
                first_pair_body, [tile, half, sds(8, ROWS, COLS, dtype=BF)], sums
            )(*chip)
            recv = swap(other, "yh")
            oth = swap(ovs, "yh")
        else:
            mine, other = kernel(pair_body, [tile, half], sums)(*chip)
            recv = swap(other, "yh")
        total, out = kernel(rows_body, [tile, half], scalars=0)(mine, recv)
        three, three_half, two_half = kernel(
            near_body, [tile, half, half], scalars=0
        )(total, along_z(out, 1), along_z(out, -1))
        (msg,) = kernel(update_body, [message])(
            s,
            three,
            along_z(two_half, 3),
            along_z(three_half, -3),
            rq,
            dq,
            b_ov,
            ov2,
            oth,
        )
    (pieces,) = kernel(pieces_body, [sds(16, 16, COLS, dtype=BF)], sums)(*chip)
    pieces = lax.all_to_all(pieces, ("yh", "z"), 0, 0, tiled=True)
    (pieces,) = kernel(last_body, [sds(16, 16, COLS)])(s, pieces, rq, dq)
    w = lax.all_to_all(pieces, ("yh", "z"), 0, 0, tiled=True).reshape(256, COLS)
    return kernel(join_body, [sds(256, O)])(s, w, swap(w, "c"))[0]


def solution(mesh):
    split = Mesh(mesh.devices.reshape(2, 8, 2, 4, 2), ("yh", "z", "c", "x", "yl"))
    placed = (
        P(AUX, VIR, None),
        P(AUX, VIR, None),
        P(AUX, None, None),
        P(VIR, None),
        P(AUX),
        P(VIR),
        P(),
    )
    return jax.shard_map(
        local, mesh=split, in_specs=placed, out_specs=P(VIR, None), check_vma=False
    )
```

```python
import math

import jax
import jax.numpy as jnp
from jax import lax
from jax.experimental import pallas as pl
from jax.experimental.pallas import tpu as pltpu
from jax.sharding import Mesh
from jax.sharding import PartitionSpec as P


V = 2048
O = 512
NAUX = 128
ITERS = 3
AUX = ("yh", "z", "c")
VIR = ("x", "yl")
PLANE = ("x", "yl", "yh")
SCALE = math.sqrt(4.0 * V * O / NAUX)
BF, F32 = jnp.bfloat16, jnp.float32
ROWS, COLS, GROWS = 128, 256, 8
PIECE = ROWS + GROWS


def sds(*shape, dtype=F32):
    return jax.ShapeDtypeStruct(shape, dtype)


def kernel(body, outputs, scratch=(), limit=8, flops=0, scalars=1, far=(), out=()):
    def call(*args):
        moved = sum(math.prod(a.shape) * jnp.dtype(a.dtype).itemsize for a in (*args, *outputs))
        return pl.pallas_call(
            body,
            out_shape=list(outputs),
            in_specs=[
                pl.BlockSpec(
                    memory_space=pltpu.SMEM
                    if k < scalars
                    else pltpu.HBM
                    if k in far
                    else pltpu.VMEM
                )
                for k in range(len(args))
            ],
            out_specs=[
                pl.BlockSpec(memory_space=pltpu.HBM if k in out else pltpu.VMEM)
                for k in range(len(outputs))
            ],
            scratch_shapes=list(scratch),
            compiler_params=pltpu.CompilerParams(vmem_limit_bytes=limit << 20),
            cost_estimate=pl.CostEstimate(
                flops=flops, bytes_accessed=moved, transcendentals=0
            ),
        )(*args)

    return call


def at(index, size):
    return pl.ds(pl.multiple_of(index * size, size), size)


def spread(sums):
    g = jnp.sum(sums, axis=1, keepdims=True)
    high = g.astype(BF)
    low = (g - high.astype(F32)).astype(BF)
    lane = lax.broadcasted_iota(jnp.int32, (GROWS, 128), 1)
    wide = (GROWS, 128)
    return jnp.where(
        lane % 2 == 0,
        jnp.broadcast_to(high.astype(F32), wide),
        jnp.broadcast_to(low.astype(F32), wide),
    )


def send_all(msg, body, left, right):
    block = jnp.concatenate([left, right], axis=1).astype(BF)
    for p in range(16):
        msg[p, :ROWS, :] = body
        msg[p, ROWS:, :] = block


def lane_sums(refs, wide):
    return jnp.concatenate(
        [jnp.sum(v.astype(F32) * wide, axis=0, keepdims=True) for v in refs], axis=0
    )


def start_body(
    s, rhs_h, ev_h, eo_h, ov_h, v_h, msg, rq, dq, v, rhs, ev, eo, ov, keep, den, sems
):
    c, yh = s[0], s[1]
    copies = [
        pltpu.make_async_copy(src, dst, sems.at[k])
        for k, (src, dst) in enumerate(
            ((ev_h, ev), (eo_h, eo), (rhs_h, rhs), (ov_h, ov), (v_h, v))
        )
    ]
    for copy in copies:
        copy.start()
    copies[0].wait()
    copies[1].wait()
    column = jnp.broadcast_to(ev[...], (128, 256)).T
    for h in range(4):
        lanes = slice(h * 128, (h + 1) * 128)
        den[:, lanes] = column - eo[:, lanes]
    copies[2].wait()
    u = (rhs[...] / den[...]).astype(BF)
    keep[...] = u
    rq[...] = rhs[at(yh, ROWS), at(c, COLS)]
    dq[...] = den[at(yh, ROWS), at(c, COLS)]
    copies[3].wait()
    sums = lane_sums([ov[q] for q in range(4)], u.astype(F32))
    sums = sums[:, :COLS] + sums[:, COLS:]
    sums = jnp.concatenate([sums, jnp.zeros((4, COLS), F32)], axis=0)
    g = spread(sums)
    zero = jnp.zeros_like(g)
    send_all(
        msg,
        keep[at(yh, ROWS), at(c, COLS)],
        jnp.where(yh == 0, g, zero),
        jnp.where(yh == 0, zero, g),
    )
    copies[4].wait()


def load_body(s, v_h, after, v, sems):
    copies = [pltpu.make_async_copy(v_h.at[q], v.at[q], sems.at[q]) for q in range(4)]
    for copy in copies:
        copy.start()
    for copy in copies:
        copy.wait()


def main_body(s, fit, v1, v2, o1, o2, u, keep, send, part, full, zs, gs, ac):
    c, yh = s[0], s[1]
    g = jnp.zeros((GROWS, COLS), F32)
    for p in range(16):
        full[p * ROWS : (p + 1) * ROWS, :] = u[p, :ROWS, :]
        g = g + u[p, ROWS:, :].astype(F32)
    gs[...] = g
    g = gs[:, at(yh, 128)]
    g = g + pltpu.roll(g, 1, 1)
    own = [jnp.full((1, 128), SCALE * fit[q], F32) for q in range(4)]
    w = jnp.concatenate([*own, jnp.zeros((4, 128), F32)], axis=0) - 4.0 * g
    part[...] = w
    send[256:, :] = jnp.concatenate([w, w], axis=1)
    for k, v in enumerate((v1, v2)):
        z = jnp.dot(
            v[...].reshape(4 * 256, V), full[...], preferred_element_type=F32
        ).astype(BF)
        for q in range(4):
            zs[:, (k * 4 + q) * 256 : (k * 4 + q + 1) * 256] = z[q * 256 : (q + 1) * 256]
    o = jnp.concatenate([r[q, at(c, 256), :] for r in (o1, o2) for q in range(4)], axis=0)
    ac[...] = jnp.dot(zs[...], o, preferred_element_type=F32)
    keep[...] = ac[:, at(c, COLS)]
    send[:256, :] = ac[:, at(1 - c, COLS)]


def chip_total(s, keep, got, part, ov, ov2, tot):
    c = s[0]
    other = got[256:, :128]
    w = part[...] + jnp.concatenate([other[4:8, :], other[0:4, :]], axis=0)
    for h in range(2):
        lanes = slice(h * 128, (h + 1) * 128)
        acc = keep[:, lanes] + got[:256, lanes]
        for q in range(8):
            ref = (ov, ov2)[q // 4]
            acc += ref[q % 4, :, at(c * 2 + h, 128)].astype(F32) * w[q : q + 1, :]
        tot[:, lanes] = acc


def pair_body(s, keep, got, part, ov, ov2, mine, other, tot):
    yh = s[1]
    chip_total(s, keep, got, part, ov, ov2, tot)
    mine[...] = tot[at(yh, ROWS), :]
    other[...] = tot[at(1 - yh, ROWS), :].astype(BF)


def rows_body(mine, recv, total, out):
    t = mine[...] + recv[...].astype(F32)
    total[...] = t
    out[...] = t.astype(BF)


def first_pair_body(s, keep, got, part, ov, ov2, mine, other, ovs, tot):
    c, yh = s[0], s[1]
    pair_body(s, keep, got, part, ov, ov2, mine, other, tot)
    for q in range(8):
        ovs[q] = (ov, ov2)[q // 4][q % 4, at(1 - yh, ROWS), at(c, COLS)]


def two_body(total, after, two, two_half):
    t = total[...] + after[...].astype(F32)
    two[...] = t
    two_half[...] = t.astype(BF)


def three_body(two, before, three, three_half):
    t = two[...] + before[...].astype(F32)
    three[...] = t
    three_half[...] = t.astype(BF)


def pieces_body(s, keep, got, part, ov, ov2, out, tot):
    chip_total(s, keep, got, part, ov, ov2, tot)
    for p in range(16):
        out[p] = tot[p * 16 : (p + 1) * 16, :].astype(BF)


def update_body(s, three, before, after, rq, dq, ov, ov2, oth, msg):
    c, yh = s[0], s[1]
    share = three[...] + before[...].astype(F32) + after[...].astype(F32)
    u = ((rq[...] + share) / dq[...]).astype(BF)
    wide = u.astype(F32)
    rows, cols = at(yh, ROWS), at(c, COLS)
    own = spread(lane_sums([r[q, rows, cols] for r in (ov, ov2) for q in range(4)], wide))
    far = spread(lane_sums([oth[q] for q in range(8)], wide))
    send_all(
        msg, u, jnp.where(yh == 0, own, far), jnp.where(yh == 0, far, own)
    )


def last_body(s, pieces, rq, dq, out):
    share = pieces[0].astype(F32)
    for p in range(1, 16):
        share += pieces[p].astype(F32)
    rows = at(s[2], 16)
    w = (rq[rows, :] + share) / dq[rows, :]
    for p in range(16):
        out[p] = w


def join_body(s, w, wc, out):
    c = s[0]
    out[:, at(c, COLS)] = w[...]
    out[:, at(1 - c, COLS)] = wc[...]


def swap(value, axis):
    return lax.ppermute(value, axis, [(0, 1), (1, 0)])


def along_z(value, shift):
    n = lax.axis_size("z")
    return lax.ppermute(value, "z", [(i, (i + shift) % n) for i in range(n)])


def local(b_ov, b_vv, b_oo, rhs, fit_pert, eps_vir, eps_occ):
    s = jnp.stack([lax.axis_index(a) for a in ("c", "yh", "z")]).astype(jnp.int32)
    tile = sds(ROWS, COLS)
    half = sds(ROWS, COLS, dtype=BF)
    message = sds(16, PIECE, COLS, dtype=BF)
    msg, rq, dq, v1 = kernel(
        start_body,
        [message, tile, tile, pltpu.VMEM((4, 256, V), BF)],
        [
            pltpu.VMEM((256, O), F32),
            pltpu.VMEM((1, 256), F32),
            pltpu.VMEM((1, O), F32),
            pltpu.VMEM((4, 256, O), BF),
            pltpu.VMEM((256, O), BF),
            pltpu.VMEM((256, O), F32),
            pltpu.SemaphoreType.DMA((5,)),
        ],
        limit=12,
        far=range(1, 6),
    )(
        s,
        *(
            pltpu.with_memory_space_constraint(a, pltpu.HBM)
            for a in (rhs, eps_vir[None, :], eps_occ[None, :], b_ov, b_vv)
        ),
    )
    vv2, oo2 = swap(b_vv, "c"), swap(b_oo, "c")
    oth = None
    for step in range(ITERS):
        msg = lax.all_to_all(msg, PLANE, 0, 0, tiled=True)
        if oth is None:
            msg, b_ov, fit_pert, s = lax.optimization_barrier((msg, b_ov, fit_pert, s))
            ov2 = swap(b_ov, "c")
            (v2,) = kernel(
                load_body, [pltpu.VMEM((4, 256, V), BF)], [pltpu.SemaphoreType.DMA((4,))], far=(1,)
            )(
                s,
                pltpu.with_memory_space_constraint(vv2, pltpu.HBM),
                msg[:1, :8, :128],
            )
        keep, send, part = kernel(
            main_body,
            [sds(256, COLS), sds(256 + 8, COLS), sds(8, 128)],
            [
                pltpu.VMEM((V, COLS), BF),
                pltpu.VMEM((256, V), BF),
                pltpu.VMEM((GROWS, COLS), F32),
                pltpu.VMEM((256, O), F32),
            ],
            limit=12,
            flops=2 * 8 * 256 * 256 * (V + O),
            scalars=2,
        )(s, fit_pert, v1, v2, b_oo, oo2, msg)
        chip = (s, keep, swap(send, "c"), part, b_ov, ov2)
        sums = [pltpu.VMEM((256, COLS), F32)]
        if step == ITERS - 1:
            break
        if oth is None:
            mine, other, ovs = kernel(
                first_pair_body, [tile, half, sds(8, ROWS, COLS, dtype=BF)], sums
            )(*chip)
            recv = swap(other, "yh")
            oth = swap(ovs, "yh")
        else:
            mine, other = kernel(pair_body, [tile, half], sums)(*chip)
            recv = swap(other, "yh")
        total, out = kernel(rows_body, [tile, half], scalars=0)(mine, recv)
        after = along_z(out, -1)
        before = along_z(out, 1)
        two, two_half = kernel(two_body, [tile, half], scalars=0)(
            total, after
        )
        far_two = along_z(two_half, 3)
        three, three_half = kernel(three_body, [tile, half], scalars=0)(
            two, before
        )
        far_three = along_z(three_half, -3)
        (msg,) = kernel(update_body, [message])(
            s,
            three,
            far_two,
            far_three,
            rq,
            dq,
            b_ov,
            ov2,
            oth,
        )
    (pieces,) = kernel(pieces_body, [sds(16, 16, COLS, dtype=BF)], sums)(*chip)
    pieces = lax.all_to_all(pieces, ("yh", "z"), 0, 0, tiled=True)
    (pieces,) = kernel(last_body, [sds(16, 16, COLS)])(s, pieces, rq, dq)
    w = lax.all_to_all(pieces, ("yh", "z"), 0, 0, tiled=True).reshape(256, COLS)
    return kernel(join_body, [sds(256, O)])(s, w, swap(w, "c"))[0]


def solution(mesh):
    split = Mesh(mesh.devices.reshape(2, 8, 2, 4, 2), ("yh", "z", "c", "x", "yl"))
    placed = (
        P(AUX, VIR, None),
        P(AUX, VIR, None),
        P(AUX, None, None),
        P(VIR, None),
        P(AUX),
        P(VIR),
        P(),
    )
    return jax.shard_map(
        local, mesh=split, in_specs=placed, out_specs=P(VIR, None), check_vma=False
    )
```

```python
import math

import jax
import jax.numpy as jnp
from jax import lax
from jax.experimental import pallas as pl
from jax.experimental.pallas import tpu as pltpu
from jax.sharding import Mesh
from jax.sharding import PartitionSpec as P


V = 2048
O = 512
NAUX = 128
ITERS = 3
AUX = ("yh", "z", "c")
VIR = ("x", "yl")
PLANE = ("x", "yl", "yh")
SCALE = math.sqrt(4.0 * V * O / NAUX)
BF, F32 = jnp.bfloat16, jnp.float32
ROWS, COLS, GROWS = 128, 256, 8
PIECE = ROWS + GROWS


def sds(*shape, dtype=F32):
    return jax.ShapeDtypeStruct(shape, dtype)


def kernel(body, outputs, scratch=(), limit=8, flops=0, scalars=1, far=(), out=()):
    def call(*args):
        moved = sum(math.prod(a.shape) * jnp.dtype(a.dtype).itemsize for a in (*args, *outputs))
        return pl.pallas_call(
            body,
            out_shape=list(outputs),
            in_specs=[
                pl.BlockSpec(
                    memory_space=pltpu.SMEM
                    if k < scalars
                    else pltpu.HBM
                    if k in far
                    else pltpu.VMEM
                )
                for k in range(len(args))
            ],
            out_specs=[
                pl.BlockSpec(memory_space=pltpu.HBM if k in out else pltpu.VMEM)
                for k in range(len(outputs))
            ],
            scratch_shapes=list(scratch),
            compiler_params=pltpu.CompilerParams(vmem_limit_bytes=limit << 20),
            cost_estimate=pl.CostEstimate(
                flops=flops, bytes_accessed=moved, transcendentals=0
            ),
        )(*args)

    return call


def at(index, size):
    return pl.ds(pl.multiple_of(index * size, size), size)


def spread(sums):
    g = jnp.sum(sums, axis=1, keepdims=True)
    high = g.astype(BF)
    low = (g - high.astype(F32)).astype(BF)
    lane = lax.broadcasted_iota(jnp.int32, (GROWS, 128), 1)
    wide = (GROWS, 128)
    return jnp.where(
        lane % 2 == 0,
        jnp.broadcast_to(high.astype(F32), wide),
        jnp.broadcast_to(low.astype(F32), wide),
    )


def send_all(msg, body, left, right):
    block = jnp.concatenate([left, right], axis=1).astype(BF)
    for p in range(16):
        msg[p, :ROWS, :] = body
        msg[p, ROWS:, :] = block


def lane_sums(refs, wide):
    return jnp.concatenate(
        [jnp.sum(v.astype(F32) * wide, axis=0, keepdims=True) for v in refs], axis=0
    )


def start_body(
    s, rhs_h, ev_h, eo_h, ov_h, v_h, msg, rq, dq, v, rhs, ev, eo, ov, keep, den, sems
):
    c, yh = s[0], s[1]
    copies = [
        pltpu.make_async_copy(src, dst, sems.at[k])
        for k, (src, dst) in enumerate(
            ((ev_h, ev), (eo_h, eo), (rhs_h, rhs), (ov_h, ov), (v_h, v))
        )
    ]
    for copy in copies:
        copy.start()
    copies[0].wait()
    copies[1].wait()
    column = jnp.broadcast_to(ev[...], (128, 256)).T
    for h in range(4):
        lanes = slice(h * 128, (h + 1) * 128)
        den[:, lanes] = column - eo[:, lanes]
    copies[2].wait()
    u = (rhs[...] / den[...]).astype(BF)
    keep[...] = u
    rq[...] = rhs[at(yh, ROWS), at(c, COLS)]
    dq[...] = den[at(yh, ROWS), at(c, COLS)]
    copies[3].wait()
    sums = lane_sums([ov[q] for q in range(4)], u.astype(F32))
    sums = sums[:, :COLS] + sums[:, COLS:]
    sums = jnp.concatenate([sums, jnp.zeros((4, COLS), F32)], axis=0)
    g = spread(sums)
    zero = jnp.zeros_like(g)
    send_all(
        msg,
        keep[at(yh, ROWS), at(c, COLS)],
        jnp.where(yh == 0, g, zero),
        jnp.where(yh == 0, zero, g),
    )
    copies[4].wait()


def load_body(s, v_h, after, v, sems):
    copies = [pltpu.make_async_copy(v_h.at[q], v.at[q], sems.at[q]) for q in range(4)]
    for copy in copies:
        copy.start()
    for copy in copies:
        copy.wait()


def main_body(s, fit, v1, v2, o1, o2, u, keep, send, part, full, zs, gs, ac):
    c, yh = s[0], s[1]
    g = jnp.zeros((GROWS, COLS), F32)
    for p in range(16):
        full[p * ROWS : (p + 1) * ROWS, :] = u[p, :ROWS, :]
        g = g + u[p, ROWS:, :].astype(F32)
    gs[...] = g
    g = gs[:, at(yh, 128)]
    g = g + pltpu.roll(g, 1, 1)
    own = [jnp.full((1, 128), SCALE * fit[q], F32) for q in range(4)]
    w = jnp.concatenate([*own, jnp.zeros((4, 128), F32)], axis=0) - 4.0 * g
    part[...] = w
    send[256:, :] = jnp.concatenate([w, w], axis=1)
    for k, v in enumerate((v1, v2)):
        z = jnp.dot(
            v[...].reshape(4 * 256, V), full[...], preferred_element_type=F32
        ).astype(BF)
        for q in range(4):
            zs[:, (k * 4 + q) * 256 : (k * 4 + q + 1) * 256] = z[q * 256 : (q + 1) * 256]
    o = jnp.concatenate([r[q, at(c, 256), :] for r in (o1, o2) for q in range(4)], axis=0)
    ac[...] = jnp.dot(zs[...], o, preferred_element_type=F32)
    keep[...] = ac[:, at(c, COLS)]
    send[:256, :] = ac[:, at(1 - c, COLS)]


def chip_total(s, keep, got, part, ov, ov2, tot):
    c = s[0]
    other = got[256:, :128]
    w = part[...] + jnp.concatenate([other[4:8, :], other[0:4, :]], axis=0)
    for h in range(2):
        lanes = slice(h * 128, (h + 1) * 128)
        acc = keep[:, lanes] + got[:256, lanes]
        for q in range(8):
            ref = (ov, ov2)[q // 4]
            acc += ref[q % 4, :, at(c * 2 + h, 128)].astype(F32) * w[q : q + 1, :]
        tot[:, lanes] = acc


def pair_body(s, keep, got, part, ov, ov2, mine, other, tot):
    yh = s[1]
    chip_total(s, keep, got, part, ov, ov2, tot)
    mine[...] = tot[at(yh, ROWS), :]
    other[...] = tot[at(1 - yh, ROWS), :].astype(BF)


def rows_body(mine, recv, total, out):
    t = mine[...] + recv[...].astype(F32)
    total[...] = t
    out[...] = t.astype(BF)


def first_pair_body(s, keep, got, part, ov, ov2, mine, other, ovs, tot):
    c, yh = s[0], s[1]
    pair_body(s, keep, got, part, ov, ov2, mine, other, tot)
    for q in range(8):
        ovs[q] = (ov, ov2)[q // 4][q % 4, at(1 - yh, ROWS), at(c, COLS)]


def two_body(total, after, two, two_half):
    t = total[...] + after[...].astype(F32)
    two[...] = t
    two_half[...] = t.astype(BF)


def three_body(two, before, three, three_half):
    t = two[...] + before[...].astype(F32)
    three[...] = t
    three_half[...] = t.astype(BF)


def pieces_body(s, keep, got, part, ov, ov2, out, tot):
    chip_total(s, keep, got, part, ov, ov2, tot)
    for p in range(16):
        out[p] = tot[p * 16 : (p + 1) * 16, :].astype(BF)


def update_body(s, three, before, after, rq, dq, ov, ov2, oth, msg):
    c, yh = s[0], s[1]
    share = three[...] + before[...].astype(F32) + after[...].astype(F32)
    u = ((rq[...] + share) / dq[...]).astype(BF)
    wide = u.astype(F32)
    rows, cols = at(yh, ROWS), at(c, COLS)
    own = spread(lane_sums([r[q, rows, cols] for r in (ov, ov2) for q in range(4)], wide))
    far = spread(lane_sums([oth[q] for q in range(8)], wide))
    send_all(
        msg, u, jnp.where(yh == 0, own, far), jnp.where(yh == 0, far, own)
    )


def last_body(pieces, out):
    share = pieces[0].astype(F32)
    for p in range(1, 16):
        share += pieces[p].astype(F32)
    share = share.astype(BF)
    for p in range(16):
        out[p] = share


def join_body(s, own, other, rhs, ev, eo, out, share):
    c = s[0]
    share[:, at(c, COLS)] = own[...].astype(F32)
    share[:, at(1 - c, COLS)] = other[...].astype(F32)
    column = jnp.broadcast_to(ev[...], (128, 256)).T
    for h in range(4):
        lanes = slice(h * 128, (h + 1) * 128)
        out[:, lanes] = (rhs[:, lanes] + share[:, lanes]) / (column - eo[:, lanes])


def swap(value, axis):
    return lax.ppermute(value, axis, [(0, 1), (1, 0)])


def along_z(value, shift):
    n = lax.axis_size("z")
    return lax.ppermute(value, "z", [(i, (i + shift) % n) for i in range(n)])


def local(b_ov, b_vv, b_oo, rhs, fit_pert, eps_vir, eps_occ):
    s = jnp.stack([lax.axis_index(a) for a in ("c", "yh", "z")]).astype(jnp.int32)
    tile = sds(ROWS, COLS)
    half = sds(ROWS, COLS, dtype=BF)
    message = sds(16, PIECE, COLS, dtype=BF)
    msg, rq, dq, v1 = kernel(
        start_body,
        [message, tile, tile, pltpu.VMEM((4, 256, V), BF)],
        [
            pltpu.VMEM((256, O), F32),
            pltpu.VMEM((1, 256), F32),
            pltpu.VMEM((1, O), F32),
            pltpu.VMEM((4, 256, O), BF),
            pltpu.VMEM((256, O), BF),
            pltpu.VMEM((256, O), F32),
            pltpu.SemaphoreType.DMA((5,)),
        ],
        limit=12,
        far=range(1, 6),
    )(
        s,
        *(
            pltpu.with_memory_space_constraint(a, pltpu.HBM)
            for a in (rhs, eps_vir[None, :], eps_occ[None, :], b_ov, b_vv)
        ),
    )
    vv2, oo2 = swap(b_vv, "c"), swap(b_oo, "c")
    oth = None
    for step in range(ITERS):
        msg = lax.all_to_all(msg, PLANE, 0, 0, tiled=True)
        if oth is None:
            msg, b_ov, fit_pert, s = lax.optimization_barrier((msg, b_ov, fit_pert, s))
            ov2 = swap(b_ov, "c")
            (v2,) = kernel(
                load_body, [pltpu.VMEM((4, 256, V), BF)], [pltpu.SemaphoreType.DMA((4,))], far=(1,)
            )(
                s,
                pltpu.with_memory_space_constraint(vv2, pltpu.HBM),
                msg[:1, :8, :128],
            )
        keep, send, part = kernel(
            main_body,
            [sds(256, COLS), sds(256 + 8, COLS), sds(8, 128)],
            [
                pltpu.VMEM((V, COLS), BF),
                pltpu.VMEM((256, V), BF),
                pltpu.VMEM((GROWS, COLS), F32),
                pltpu.VMEM((256, O), F32),
            ],
            limit=12,
            flops=2 * 8 * 256 * 256 * (V + O),
            scalars=2,
        )(s, fit_pert, v1, v2, b_oo, oo2, msg)
        chip = (s, keep, swap(send, "c"), part, b_ov, ov2)
        sums = [pltpu.VMEM((256, COLS), F32)]
        if step == ITERS - 1:
            break
        if oth is None:
            mine, other, ovs = kernel(
                first_pair_body, [tile, half, sds(8, ROWS, COLS, dtype=BF)], sums
            )(*chip)
            recv = swap(other, "yh")
            oth = swap(ovs, "yh")
        else:
            mine, other = kernel(pair_body, [tile, half], sums)(*chip)
            recv = swap(other, "yh")
        total, out = kernel(rows_body, [tile, half], scalars=0)(mine, recv)
        after = along_z(out, -1)
        before = along_z(out, 1)
        two, two_half = kernel(two_body, [tile, half], scalars=0)(
            total, after
        )
        far_two = along_z(two_half, 3)
        three, three_half = kernel(three_body, [tile, half], scalars=0)(
            two, before
        )
        far_three = along_z(three_half, -3)
        (msg,) = kernel(update_body, [message])(
            s,
            three,
            far_two,
            far_three,
            rq,
            dq,
            b_ov,
            ov2,
            oth,
        )
    (pieces,) = kernel(pieces_body, [sds(16, 16, COLS, dtype=BF)], sums)(*chip)
    pieces = lax.all_to_all(pieces, ("yh", "z"), 0, 0, tiled=True)
    (pieces,) = kernel(last_body, [sds(16, 16, COLS, dtype=BF)], scalars=0)(
        pieces
    )
    own = lax.all_to_all(pieces, ("yh", "z"), 0, 0, tiled=True).reshape(256, COLS)
    return kernel(join_body, [sds(256, O)], [pltpu.VMEM((256, O), F32)])(
        s, own, swap(own, "c"), rhs, eps_vir[None, :], eps_occ[None, :]
    )[0]


def solution(mesh):
    split = Mesh(mesh.devices.reshape(2, 8, 2, 4, 2), ("yh", "z", "c", "x", "yl"))
    placed = (
        P(AUX, VIR, None),
        P(AUX, VIR, None),
        P(AUX, None, None),
        P(VIR, None),
        P(AUX),
        P(VIR),
        P(),
    )
    return jax.shard_map(
        local, mesh=split, in_specs=placed, out_specs=P(VIR, None), check_vma=False
    )
```
